768 devices in a mesh: gx: 48 (over z, x_hi, core), gy: 16 (over y, x_lo).
Axes of the slice: x: 4 (x_hi: 2, x_lo: 2; x = x_hi * 2 + x_lo), y: 8, z: 12, core: 2. Of those that a mesh axis runs over, the one named last changes fastest.
Arguments:
- e_field: float32 [3, 384, 128, 128], P(None, 'gx', 'gy'), may hold values from -6 to 6
- h_field: float32 [3, 384, 128, 128], P(None, 'gx', 'gy'), may hold values from -6 to 6
- current: float32 [3, 384, 128, 128], P(None, 'gx', 'gy'), may hold values from -4 to 4
- material: int32 [384, 128, 128], P('gx', 'gy'), may hold values from 0 to 7
- pole: int32 [384, 128, 128], P('gx', 'gy'), may hold values from 0 to 3
- permittivity: float32 [8], replicated, may hold values from 1 to 6
- conductivity: float32 [8], replicated, may hold values from 0.05 to 1
- plasma: float32 [4], replicated, may hold values from 0.1 to 2
- damping: float32 [4], replicated, may hold values from 0.05 to 1
- box: int32 [4], replicated, may hold values from 1 to 383, as said below
- spectral_slot: int32 [128], replicated, may hold values from 0 to 511
- ux_index: int32 [48], replicated, may hold values from 0 to 255
- uz_index: int32 [16], replicated, may hold values from 0 to 255
Outputs:
- e_final: float32 [3, 384, 128, 128], P(None, 'gx', 'gy')
- h_final: float32 [3, 384, 128, 128], P(None, 'gx', 'gy')
- current_final: float32 [3, 384, 128, 128], P(None, 'gx', 'gy')
- far_field: float32 [4, 48, 16, 128], P(None, 'gx', 'gy')
The draws below stay inside these ranges and needn't reach their ends.
Inputs may be any that keep to these rules, and one draw needn't show every extreme that they name: box[0] = 1, box[1] = 383, 1 <= box[2] <= 32 and 96 <= box[3] <= 127.
All inputs are finite; a program needn't handle non-finite values.
Results may differ from the reference program's by a relative error of at most 0.0003.
Values sent between devices are 32-bit elements; how exact they have to be, the bound alone decides.
A program may use at most 32 MiB of HBM per device.

```python
import math
import jax
import jax.numpy as jnp
from jax import lax

NZ = 128
MARCH_TOTAL = 3
F = 128
SPECTRUM_POINTS = 512
AGRID = 256
MATS = 8
POLES = 4
NX = 384
NY = 128
I = 48
J = 16


def draw_box(key, part):
    keys = jax.random.split(jax.random.fold_in(key, 17), 4)
    first_x = jax.random.randint(keys[0], (), 1, NX // 4 + 1)
    end_x = jax.random.randint(keys[1], (), 3 * NX // 4, NX)
    lower_y = jax.random.randint(keys[2], (), 1, NY // 4 + 1)
    upper_y = jax.random.randint(keys[3], (), 3 * NY // 4, NY)
    if NX >= NY:
        first_x = jnp.ones((), jnp.int32)
        end_x = jnp.full((), NX - 1, jnp.int32)
    else:
        lower_y = jnp.ones((), jnp.int32)
        upper_y = jnp.full((), NY - 1, jnp.int32)
    return jnp.stack([first_x, end_x, lower_y, upper_y]).astype(jnp.int32)


def with_ends(entries, rng, low, largest):
    longest = entries.shape.index(max(entries.shape))
    spots = []
    for shift in (0, 1):
        where = [jax.random.randint(jax.random.fold_in(rng, axis), (), 0, length) for axis, length in enumerate(entries.shape)]
        where[longest] = (where[longest] + shift) % entries.shape[longest]
        spots.append(tuple(where))
    return entries.at[spots[0]].set(low).at[spots[1]].set(largest)


def block_scale(key, dims, pieces, low, top_value):
    def one(dim, blocks):
        steps = jax.random.uniform(jax.random.fold_in(jax.random.fold_in(key, 6), dim), (blocks,), jnp.float32, low / len(pieces), top_value / len(pieces))
        return jnp.repeat(jnp.exp(steps), dims[dim] // blocks).reshape((-1,) + (1,) * (len(dims) - dim - 1))

    gain = one(*pieces[0])
    for cut in pieces[1:]:
        gain = gain * one(*cut)
    return gain


def centred(key, dims, spread, limit, pieces=(), held_as=jnp.bfloat16):
    level = block_scale(key, dims, pieces, -0.22, 0.18) if pieces else 1.0
    drawn = jax.random.normal(key, dims, jnp.float32) * spread * level
    return jnp.minimum(jnp.maximum(drawn, -limit), limit).astype(held_as)


def setup_inputs(seed: int = 0) -> dict:
    arg_keys = jax.random.split(jax.random.key(seed), 14)
    e_field = centred(arg_keys[0], (3, NX, NY, NZ), 1.0, 6.0, ((1, 48), (2, 16)), jnp.float32)
    h_field = centred(arg_keys[1], (3, NX, NY, NZ), 1.0, 6.0, ((1, 48), (2, 16)), jnp.float32)
    current = centred(arg_keys[2], (3, NX, NY, NZ), 0.5, 4.0, ((1, 48), (2, 16)), jnp.float32)
    material = with_ends(jax.random.randint(arg_keys[3], (NX, NY, NZ), 0, MATS), jax.random.fold_in(arg_keys[3], 1), 0, MATS - 1).astype(jnp.int32)
    pole = with_ends(jax.random.randint(arg_keys[4], (NX, NY, NZ), 0, POLES), jax.random.fold_in(arg_keys[4], 1), 0, POLES - 1).astype(jnp.int32)
    permittivity = jnp.clip(jnp.exp(jax.random.uniform(arg_keys[5], (MATS,), jnp.float32, math.log(1.0), math.log(6.0))), 1.0, 6.0)
    conductivity = jnp.clip(jnp.exp(jax.random.uniform(arg_keys[6], (MATS,), jnp.float32, math.log(0.05), math.log(1.0))), 0.05, 1.0)
    plasma = jnp.clip(jnp.exp(jax.random.uniform(arg_keys[7], (POLES,), jnp.float32, math.log(0.1), math.log(2.0))), 0.1, 2.0)
    damping = jnp.clip(jnp.exp(jax.random.uniform(arg_keys[8], (POLES,), jnp.float32, math.log(0.05), math.log(1.0))), 0.05, 1.0)
    box = draw_box(jax.random.fold_in(arg_keys[13], 71), 0)
    spectral_slot = with_ends(jax.random.randint(arg_keys[10], (F,), 0, SPECTRUM_POINTS), jax.random.fold_in(arg_keys[10], 1), 0, SPECTRUM_POINTS - 1).astype(jnp.int32)
    ux_index = with_ends(jax.random.randint(arg_keys[11], (I,), 0, AGRID), jax.random.fold_in(arg_keys[11], 1), 0, AGRID - 1).astype(jnp.int32)
    uz_index = with_ends(jax.random.randint(arg_keys[12], (J,), 0, AGRID), jax.random.fold_in(arg_keys[12], 1), 0, AGRID - 1).astype(jnp.int32)
    return dict(e_field=e_field, h_field=h_field, current=current, material=material, pole=pole, permittivity=permittivity, conductivity=conductivity, plasma=plasma, damping=damping, box=box, spectral_slot=spectral_slot, ux_index=ux_index, uz_index=uz_index)


delta_interval = 0.5
highest = lax.Precision.HIGHEST

def ahead(values, axis):
    padding = [(0, 0)] * values.ndim
    padding[axis] = (0, 1)
    padded = jnp.pad(values, padding)
    return lax.slice_in_dim(padded, 1, values.shape[axis] + 1, axis=axis) - values

def behind(values, axis):
    padding = [(0, 0)] * values.ndim
    padding[axis] = (1, 0)
    padded = jnp.pad(values, padding)
    return values - lax.slice_in_dim(padded, 0, values.shape[axis], axis=axis)

def curl_e(field):
    return jnp.stack([ahead(field[2], 1) - ahead(field[1], 2), ahead(field[0], 2) - ahead(field[2], 0), ahead(field[1], 0) - ahead(field[0], 1)])

def curl_h(field):
    return jnp.stack([behind(field[2], 1) - behind(field[1], 2), behind(field[0], 2) - behind(field[2], 0), behind(field[1], 0) - behind(field[0], 1)])

def surface(e_field, h_field, box, inside_x):
    sheets = []
    for position, sign in ((2, -1.0), (3, 1.0)):
        e_row = lax.dynamic_index_in_dim(e_field, box[position], axis=2, keepdims=False)
        h_row = lax.dynamic_index_in_dim(h_field, box[position], axis=2, keepdims=False)
        quantity = jnp.stack([h_row[2], -h_row[0], -e_row[2], e_row[0]])
        sheets.append(sign * quantity * inside_x[None, :, None])
    return jnp.stack(sheets)

def reference(e_field, h_field, current, material, pole, permittivity, conductivity, plasma, damping, box, spectral_slot, ux_index, uz_index):
    dielectric_voxel = permittivity[material]
    sig_cell = conductivity[material]
    plasma_cell = plasma[pole]
    rate_cell = damping[pole]
    loss_term = sig_cell * delta_interval / (2.0 * dielectric_voxel)
    keep_e = (1.0 - loss_term) / (1.0 + loss_term)
    drive_e = delta_interval / dielectric_voxel / (1.0 + loss_term)
    half_rate = rate_cell * delta_interval / 2.0
    keep_j = (1.0 - half_rate) / (1.0 + half_rate)
    drive_j = plasma_cell * delta_interval / (1.0 + half_rate)
    x_cells = jnp.arange(NX)
    inside_x = ((x_cells >= box[0]) & (x_cells < box[1])).astype(jnp.float32)
    records = []
    for step_index in range(MARCH_TOTAL):
        current = keep_j * current + drive_j * e_field
        e_field = keep_e * e_field + drive_e * (curl_h(h_field) - current)
        h_field = h_field - delta_interval * curl_e(e_field)
        records.append(surface(e_field, h_field, box, inside_x))
    stacked = jnp.stack(records, axis=1)
    drive_pulsation = math.pi * (spectral_slot.astype(jnp.float32) + 0.5) / SPECTRUM_POINTS
    heading_first = -0.7 + 1.4 * (ux_index.astype(jnp.float32) + 0.5) / AGRID
    heading_third = -0.7 + 1.4 * (uz_index.astype(jnp.float32) + 0.5) / AGRID
    heading_second = jnp.sqrt(1.0 - heading_first[:, None] ** 2 - heading_third[None, :] ** 2)
    tick_epochs = jnp.arange(1, MARCH_TOTAL + 1).astype(jnp.float32) * delta_interval
    first_location = (jnp.arange(NX) - NX // 2).astype(jnp.float32)
    third_location = (jnp.arange(NZ) - NZ // 2).astype(jnp.float32)
    second_location = (box[2:4] - NY // 2).astype(jnp.float32)

    def single_spectral_line(omega_value):
        cycle_exponent = omega_value * tick_epochs
        d_real = jnp.einsum('n,pncxz->pcxz', jnp.cos(cycle_exponent), stacked, precision=highest)
        d_imag = -jnp.einsum('n,pncxz->pcxz', jnp.sin(cycle_exponent), stacked, precision=highest)
        third_bearing = (omega_value * heading_third)[None, :] * third_location[:, None]
        cos_z, sin_z = (jnp.cos(third_bearing), jnp.sin(third_bearing))
        a_real = jnp.einsum('pcxz,zj->pcxj', d_real, cos_z, precision=highest) - jnp.einsum('pcxz,zj->pcxj', d_imag, sin_z, precision=highest)
        a_imag = jnp.einsum('pcxz,zj->pcxj', d_real, sin_z, precision=highest) + jnp.einsum('pcxz,zj->pcxj', d_imag, cos_z, precision=highest)
        first_bearing = (omega_value * heading_first)[None, :] * first_location[:, None]
        cos_x, sin_x = (jnp.cos(first_bearing), jnp.sin(first_bearing))
        b_real = jnp.einsum('pcxj,xi->pcij', a_real, cos_x, precision=highest) - jnp.einsum('pcxj,xi->pcij', a_imag, sin_x, precision=highest)
        b_imag = jnp.einsum('pcxj,xi->pcij', a_real, sin_x, precision=highest) + jnp.einsum('pcxj,xi->pcij', a_imag, cos_x, precision=highest)
        second_bearing = (omega_value * heading_second)[None] * second_location[:, None, None]
        cos_y, sin_y = (jnp.cos(second_bearing), jnp.sin(second_bearing))
        refractive_real = lax.optimization_barrier(jnp.sum(b_real * cos_y[:, None] - b_imag * sin_y[:, None], axis=0))
        n_imag = lax.optimization_barrier(jnp.sum(b_real * sin_y[:, None] + b_imag * cos_y[:, None], axis=0))
        return jnp.stack([refractive_real, n_imag])
    emitted_pattern = jnp.moveaxis(lax.map(single_spectral_line, drive_pulsation), 0, -1)
    sine_theta = jnp.sqrt(1.0 - heading_third ** 2)
    ratio_a = (heading_first[:, None] * heading_third[None, :] / sine_theta[None, :])[:, :, None]
    ratio_b = (heading_second / sine_theta[None, :])[:, :, None]
    sine = sine_theta[None, :, None]
    parts = []
    for which in range(2):
        block = emitted_pattern[which]
        parts.append((block[2] * ratio_b - block[0] * ratio_a + block[1] * sine) / math.sqrt(NX * NZ))
        parts.append((block[2] * ratio_a - block[3] * sine + block[0] * ratio_b) / math.sqrt(NX * NZ))
    far_field = jnp.stack([parts[0], parts[2], parts[1], parts[3]])
    return (e_field, h_field, current, far_field)
```

```python
import math

import jax
import jax.numpy as jnp
from jax import lax
from jax.experimental import pallas as pl
from jax.experimental.pallas import tpu as pltpu
from jax.sharding import PartitionSpec as P

STEPS = 3
SPECTRUM_POINTS = 512
AGRID = 256
DT = 0.5
MESH = pl.DeviceIdType.MESH
F32 = jnp.float32
HIGHEST = lax.Precision.HIGHEST
TWO_OVER_PI = 0.6366197723675814
HALF_PI_HIGH = 1.5703125
HALF_PI_LOW = 4.838267948966e-4


def sincos(angle):
    turns = jnp.round(angle * TWO_OVER_PI)
    rest = (angle - turns * HALF_PI_HIGH) - turns * HALF_PI_LOW
    square = rest * rest
    sine = rest + rest * square * (
        -1.6666654611e-1 + square * (8.3321608736e-3 + square * -1.9515295891e-4)
    )
    cosine = (
        1.0
        - 0.5 * square
        + square
        * square
        * (4.166664568298827e-2 + square * (-1.388731625493765e-3 + square * 2.443315711809948e-5))
    )
    quadrant = turns.astype(jnp.int32)
    odd = (quadrant & 1) != 0
    sine_part = jnp.where(odd, cosine, sine)
    cosine_part = jnp.where(odd, sine, cosine)
    sine_out = jnp.where((quadrant & 2) != 0, -sine_part, sine_part)
    cosine_out = jnp.where(((quadrant + 1) & 2) != 0, -cosine_part, cosine_part)
    return cosine_out, sine_out


def make_kernel(sizes):
    gx_count, gy_count, cx, cy, depth, freqs, dirs_x = sizes
    half = cx
    tiles = dirs_x // 8

    def kernel(
        e_in,
        h_in,
        j_in,
        m_in,
        p_in,
        permittivity,
        conductivity,
        plasma,
        damping,
        box,
        ux_index,
        uz_index,
        slot,
        e_out,
        h_out,
        j_out,
        far_out,
        E,
        H,
        J,
        M,
        Q,
        K,
        S,
        R,
        C,
        G,
        A,
        TZ,
        TX,
        TY,
        PART,
        RX,
        local_sem,
        halo_send,
        halo_recv,
        rs_send,
        rs_recv,
        ag_send,
        ag_recv,
        gx_send,
        gx_recv,
    ):
        gx = lax.axis_index("gx")
        gy = lax.axis_index("gy")
        left = lax.rem(gx + gx_count - 1, gx_count)
        right = lax.rem(gx + 1, gx_count)
        below = lax.rem(gy + gy_count - 1, gy_count)
        above = lax.rem(gy + 1, gy_count)
        side = lax.div(gy, half)
        member = lax.rem(gy, half)

        own = (slice(None), pl.ds(0, cx), pl.ds(0, cy))
        local = [
            pltpu.make_async_copy(e_in, E.at[:, 0:cx, 0:cy, :], local_sem.at[0]),
            pltpu.make_async_copy(h_in, H.at[0, :, 0:cx, 0:cy, :], local_sem.at[1]),
            pltpu.make_async_copy(j_in, J.at[:, 0:cx, 0:cy, :], local_sem.at[2]),
            pltpu.make_async_copy(m_in, M.at[0:cx, 0:cy, :], local_sem.at[3]),
            pltpu.make_async_copy(p_in, Q.at[0:cx, 0:cy, :], local_sem.at[4]),
        ]
        for copy in local:
            copy.start()

        barrier = pltpu.get_barrier_semaphore()
        for place in ((left, above), (right, below)):
            pl.semaphore_signal(barrier, inc=1, device_id=place, device_id_type=MESH)

        def greet_row(step, carry):
            place = (lax.rem(gx + step, gx_count), gy)
            pl.semaphore_signal(barrier, inc=1, device_id=place, device_id_type=MESH)
            return carry

        def greet_column(step, carry):
            place = (gx, lax.rem(gy + step, gy_count))
            pl.semaphore_signal(barrier, inc=1, device_id=place, device_id_type=MESH)
            return carry

        lax.fori_loop(1, gy_count, greet_column, 0)
        lax.fori_loop(1, gx_count, greet_row, 0)

        omega = math.pi * (slot[...].astype(F32) + 0.5) / SPECTRUM_POINTS
        uz_own = -0.7 + 1.4 * (jnp.full((1, freqs), uz_index[gy], jnp.int32).astype(F32) + 0.5) / AGRID
        place_z = (lax.broadcasted_iota(jnp.int32, (depth, freqs), 0) - depth // 2).astype(F32)
        cos_z, sin_z = sincos((omega * uz_own) * place_z)
        TZ[:, 0:freqs] = cos_z
        TZ[:, freqs:] = sin_z

        sublane = lax.broadcasted_iota(jnp.int32, (8, freqs), 0)
        ux_tiles = []
        for tile in range(tiles):
            labels = jnp.zeros((8, freqs), jnp.int32)
            for row in range(8):
                labels = jnp.where(sublane == row, ux_index[tile * 8 + row], labels)
            ux_tiles.append(labels)
        ux = -0.7 + 1.4 * (jnp.concatenate(ux_tiles, axis=0).astype(F32) + 0.5) / AGRID
        omega_ux = omega * ux

        def fill_x(cell, carry):
            place_x = jnp.full((1, 1), gx * cx + cell - (gx_count * cx) // 2, jnp.int32).astype(F32)
            cos_x, sin_x = sincos(omega_ux * place_x)
            TX[0, cell] = cos_x
            TX[1, cell] = sin_x
            return carry

        lax.fori_loop(0, cx, fill_x, 0)
        uy = jnp.sqrt(1.0 - ux**2 - uz_own**2)
        for face in range(2):
            place_y = jnp.full((1, 1), box[2 + face] - (gy_count * cy) // 2, jnp.int32).astype(F32)
            cos_y, sin_y = sincos((omega * uy) * place_y)
            TY[face, 0] = cos_y
            TY[face, 1] = sin_y

        for copy in local:
            copy.wait()
        pl.semaphore_wait(barrier, gx_count - 1 + gy_count - 1 + 2)

        def halo(level):
            field = H.at[level]
            routes = [
                (field.at[:, 0, 0:cy, :], field.at[:, cx, 0:cy, :], (left, gy)),
                (field.at[:, cx - 1, 0:cy, :], field.at[:, cx + 1, 0:cy, :], (right, gy)),
                (field.at[:, 0:cx, 0, :], field.at[:, 0:cx, cy, :], (gx, below)),
                (field.at[:, 0:cx, cy - 1, :], field.at[:, 0:cx, 2 * cy - 1, :], (gx, above)),
                (field.at[0, 0, cy - 1, :], field.at[0, cx, 2 * cy - 1, :], (left, above)),
                (field.at[1, cx - 1, 0, :], field.at[1, cx + 1, cy, :], (right, below)),
            ]
            if level == 0:
                for ref in (E, J):
                    routes.append((ref.at[:, 0, 0:cy, :], ref.at[:, cx, 0:cy, :], (left, gy)))
                    routes.append((ref.at[:, 0:cx, 0, :], ref.at[:, 0:cx, cy, :], (gx, below)))
                for ref in (M, Q):
                    routes.append((ref.at[0, 0:cy, :], ref.at[cx, 0:cy, :], (left, gy)))
                    routes.append((ref.at[0:cx, 0, :], ref.at[0:cx, cy, :], (gx, below)))
            copies = []
            for index, (source, target, place) in enumerate(routes):
                copy = pltpu.make_async_remote_copy(
                    src_ref=source,
                    dst_ref=target,
                    send_sem=halo_send.at[level, index],
                    recv_sem=halo_recv.at[level, index],
                    device_id=place,
                    device_id_type=MESH,
                )
                copy.start()
                copies.append(copy)
            return copies

        pending = halo(0)

        planes, rows = cx + 1, 2 * cy
        row = lax.broadcasted_iota(jnp.int32, (1, rows, depth), 1)
        lane = lax.broadcasted_iota(jnp.int32, (1, 1, depth), 2)
        first_row = (row == 0) & (gy == 0)
        outer_row = (row >= cy) & (gy == gy_count - 1)

        def prev_y(value):
            return jnp.where(first_row, 0.0, pltpu.roll(value, 1, 1))

        def prev_z(value):
            return jnp.where(lane == 0, 0.0, pltpu.roll(value, 1, 2))

        def next_z(value):
            return jnp.where(lane == depth - 1, 0.0, pltpu.roll(value, depth - 1, 2))

        table_row = lax.broadcasted_iota(jnp.int32, (8, depth), 0)

        def table(source, count):
            values = jnp.ones((8, depth), F32)
            for entry in range(count):
                values = jnp.where(table_row == entry, source[entry], values)
            return values

        eps_table = table(permittivity, 8)
        sig_table = table(conductivity, 8)
        plasma_table = table(plasma, 4)
        damping_table = table(damping, 4)
        loss = sig_table * DT / (2.0 * eps_table)
        keep_e_table = (1.0 - loss) / (1.0 + loss)
        drive_e_table = DT / eps_table / (1.0 + loss)
        rate = damping_table * DT / 2.0
        keep_j_table = (1.0 - rate) / (1.0 + rate)
        drive_j_table = plasma_table * DT / (1.0 + rate)

        y_row = lax.broadcasted_iota(jnp.int32, (1, cy, depth), 1) + gy * cy
        face_weight = jnp.where(y_row == box[3], 1.0, 0.0) - jnp.where(y_row == box[2], 1.0, 0.0)
        x_cell = lax.broadcasted_iota(jnp.int32, (cx, depth), 0) + gx * cx
        inside = jnp.where((x_cell >= box[0]) & (x_cell < box[1]), 1.0, 0.0)

        def scatter(step):
            copies = []
            for offset in range(1, half):
                other = lax.rem(member + offset, half)
                copy = pltpu.make_async_remote_copy(
                    src_ref=S.at[step, :, pl.ds(other, 1), :],
                    dst_ref=R.at[step, :, pl.ds(member, 1), :],
                    send_sem=rs_send.at[step, offset],
                    recv_sem=rs_recv.at[step, offset],
                    device_id=(gx, side * half + other),
                    device_id_type=MESH,
                )
                copy.start()
                copies.append(copy)
            R[step, :, pl.ds(member, 1), :] = S[step, :, pl.ds(member, 1), :]
            return copies

        def gather(step):
            total = jnp.sum(R[step], axis=1, keepdims=True)
            C[step, :, 0:1, :] = total
            copies = []
            for offset in range(1, gy_count):
                other = lax.rem(gy + offset, gy_count)
                copy = pltpu.make_async_remote_copy(
                    src_ref=C.at[step, :, pl.ds(0, 1), :],
                    dst_ref=G.at[step, :, pl.ds(gy, 1), :],
                    send_sem=ag_send.at[step, offset],
                    recv_sem=ag_recv.at[step, offset],
                    device_id=(gx, other),
                    device_id_type=MESH,
                )
                copy.start()
                copies.append(copy)
            G[step, :, pl.ds(gy, 1), :] = total
            return copies

        scatters = []
        gathers = []
        halos = []
        for step in range(STEPS):
            for copy in pending:
                copy.wait_recv()
            if step == 0:
                for copy in pending[6:10]:
                    copy.wait_send()
                halos.extend(pending[:6] + pending[10:])
            else:
                halos.extend(pending)
            if step == 0:
                material = M[...]
                pole = Q[...]
                plane = lax.broadcasted_iota(jnp.int32, (planes, rows, depth), 0)
                outside = outer_row | ((plane == cx) & (gx == gx_count - 1))
                keep_e = jnp.zeros((planes, rows, depth), F32)
                drive_e = jnp.zeros((planes, rows, depth), F32)
                for entry in range(8):
                    hit = material == entry
                    keep_e = jnp.where(hit, keep_e_table[entry : entry + 1, :][None], keep_e)
                    drive_e = jnp.where(hit, drive_e_table[entry : entry + 1, :][None], drive_e)
                keep_j = jnp.zeros((planes, rows, depth), F32)
                drive_j = jnp.zeros((planes, rows, depth), F32)
                for entry in range(4):
                    hit = pole == entry
                    keep_j = jnp.where(hit, keep_j_table[entry : entry + 1, :][None], keep_j)
                    drive_j = jnp.where(hit, drive_j_table[entry : entry + 1, :][None], drive_j)
                K[0] = jnp.where(outside, 0.0, keep_e)
                K[1] = jnp.where(outside, 0.0, drive_e)
                K[2] = keep_j
                K[3] = drive_j
            hx = H[step, 0, 0:planes]
            hy = H[step, 1, 0:planes]
            hz = H[step, 2, 0:planes]
            edge_y = jnp.where(gx == 0, 0.0, H[step, 1, planes : planes + 1])
            edge_z = jnp.where(gx == 0, 0.0, H[step, 2, planes : planes + 1])
            hy_x = jnp.concatenate([edge_y, hy[0 : planes - 1]], axis=0)
            hz_x = jnp.concatenate([edge_z, hz[0 : planes - 1]], axis=0)
            curls = (
                hz - prev_y(hz) - (hy - prev_z(hy)),
                hx - prev_z(hx) - (hz - hz_x),
                hy - hy_x - (hx - prev_y(hx)),
            )
            fresh = []
            for axis in range(3):
                old = E[axis]
                flow = K[2] * J[axis] + K[3] * old
                J[axis] = flow
                value = K[0] * old + K[1] * (curls[axis] - flow)
                E[axis] = value
                fresh.append(value)
            ex, ey, ez = fresh
            ex_o, ey_o, ez_o = (value[0:cx, 0:cy] for value in fresh)
            ex_y = pltpu.roll(ex, rows - 1, 1)[0:cx, 0:cy]
            ez_y = pltpu.roll(ez, rows - 1, 1)[0:cx, 0:cy]
            ey_x = ey[1 : cx + 1, 0:cy]
            ez_x = ez[1 : cx + 1, 0:cy]
            first = ez_y - ez_o - (next_z(ey_o) - ey_o)
            second = next_z(ex_o) - ex_o - (ez_x - ez_o)
            third = ey_x - ey_o - (ex_y - ex_o)
            new_h = []
            for axis, turn in enumerate((first, second, third)):
                value = H[step, axis, 0:cx, 0:cy] - DT * turn
                H[step + 1, axis, 0:cx, 0:cy] = value
                new_h.append(value)
            if step + 1 < STEPS:
                pending = halo(step + 1)
            for index, value in enumerate((new_h[2], -new_h[0], -ez_o, ex_o)):
                S[step, index] = jnp.sum(value * face_weight, axis=1) * inside
            scatters.append(scatter(step))
            if step > 0:
                for copy in scatters[step - 1]:
                    copy.wait_recv()
                gathers.append(gather(step - 1))
        results = [
            pltpu.make_async_copy(E.at[:, 0:cx, 0:cy, :], e_out, local_sem.at[0]),
            pltpu.make_async_copy(H.at[STEPS, :, 0:cx, 0:cy, :], h_out, local_sem.at[1]),
            pltpu.make_async_copy(J.at[:, 0:cx, 0:cy, :], j_out, local_sem.at[2]),
        ]
        for copy in results:
            copy.start()
        for copy in scatters[STEPS - 1]:
            copy.wait_recv()
        gathers.append(gather(STEPS - 1))

        real = [jnp.zeros((8, freqs), F32) for _ in range(8)]
        imag = [jnp.zeros((8, freqs), F32) for _ in range(8)]
        for step in range(STEPS):
            for copy in gathers[step]:
                copy.wait_recv()
            lines = jnp.dot(
                G[step].reshape(4 * gy_count, depth),
                TZ[...],
                precision=HIGHEST,
                preferred_element_type=F32,
            )
            cos_t, sin_t = sincos(omega * ((step + 1) * DT))
            for index in range(8):
                along_cos = lines[index * 8 : index * 8 + 8, 0:freqs]
                along_sin = lines[index * 8 : index * 8 + 8, freqs:]
                real[index] = real[index] + (along_cos * cos_t + along_sin * sin_t)
                imag[index] = imag[index] + (along_sin * cos_t - along_cos * sin_t)
        for index in range(8):
            A[index, 0] = real[index]
            A[index, 1] = imag[index]

        sine_theta = jnp.sqrt(1.0 - uz_own**2)
        scale = 1.0 / math.sqrt(gx_count * cx * depth)
        uz_over = uz_own / sine_theta
        inverse = 1.0 / sine_theta

        def project(tile, carry):
            start = pl.multiple_of(tile * 8, 8)
            span = pl.ds(start, 8)
            sums = []
            for index in range(8):
                total_re = jnp.zeros((8, freqs), F32)
                total_im = jnp.zeros((8, freqs), F32)
                for cell in range(cx):
                    a_re = A[index, 0, cell : cell + 1, :]
                    a_im = A[index, 1, cell : cell + 1, :]
                    c = TX[0, cell, span, :]
                    s = TX[1, cell, span, :]
                    total_re = total_re + (a_re * c - a_im * s)
                    total_im = total_im + (a_re * s + a_im * c)
                sums.append((total_re, total_im))
            turned = []
            for comp in range(4):
                out_re = jnp.zeros((8, freqs), F32)
                out_im = jnp.zeros((8, freqs), F32)
                for face in range(2):
                    value_re, value_im = sums[comp * 2 + face]
                    c = TY[face, 0, span, :]
                    s = TY[face, 1, span, :]
                    out_re = out_re + (value_re * c - value_im * s)
                    out_im = out_im + (value_re * s + value_im * c)
                turned.append((out_re * scale, out_im * scale))
            ux_here = TX[2, 0, span, :]
            uy_here = TX[2, 1, span, :]
            ratio_a = ux_here * uz_over
            ratio_b = uy_here * inverse
            for part in range(2):
                nx, nz, lx, lz = (turned[comp][part] for comp in range(4))
                PART[part, span, :] = lx * ratio_b - nx * ratio_a + nz * sine_theta
                PART[2 + part, span, :] = lx * ratio_a - lz * sine_theta + nx * ratio_b
            return carry

        TX[2, 0] = ux + jnp.zeros((dirs_x, freqs), F32)
        TX[2, 1] = uy
        lax.fori_loop(0, tiles, project, 0)

        def exchange(step):
            other = lax.rem(gx + step, gx_count)
            return pltpu.make_async_remote_copy(
                src_ref=PART.at[:, pl.ds(other, 1), :],
                dst_ref=RX.at[:, pl.ds(gx, 1), :],
                send_sem=gx_send.at[step],
                recv_sem=gx_recv.at[step],
                device_id=(other, gy),
                device_id_type=MESH,
            )

        def send(step, carry):
            exchange(step).start()
            return carry

        def receive(step, carry):
            exchange(step).wait_recv()
            return carry

        def finish(step, carry):
            exchange(step).wait_send()
            return carry

        lax.fori_loop(1, gx_count, send, 0)
        RX[:, pl.ds(gx, 1), :] = PART[:, pl.ds(gx, 1), :]
        for group in halos, *scatters, *gathers:
            for copy in group:
                copy.wait_send()
        for copy in results:
            copy.wait()
        lax.fori_loop(1, gx_count, receive, 0)
        far_out[...] = jnp.sum(RX[...], axis=1, keepdims=True)
        lax.fori_loop(1, gx_count, finish, 0)

    return kernel


def solution(mesh):
    gx_count = mesh.shape["gx"]
    gy_count = mesh.shape["gy"]

    def body(
        e_field,
        h_field,
        current,
        material,
        pole,
        permittivity,
        conductivity,
        plasma,
        damping,
        box,
        spectral_slot,
        ux_index,
        uz_index,
    ):
        _, cx, cy, depth = e_field.shape
        freqs = spectral_slot.shape[0]
        dirs_x = ux_index.shape[0]
        anywhere = pl.BlockSpec(memory_space=pl.ANY)
        scalars = pl.BlockSpec(memory_space=pltpu.SMEM)
        vectors = pl.BlockSpec(memory_space=pltpu.VMEM)
        field = jax.ShapeDtypeStruct(e_field.shape, F32)
        e_field, h_field, current, far = pl.pallas_call(
            make_kernel((gx_count, gy_count, cx, cy, depth, freqs, dirs_x)),
            out_shape=(field, field, field, jax.ShapeDtypeStruct((4, 1, freqs), F32)),
            in_specs=[anywhere] * 5 + [scalars] * 7 + [vectors],
            out_specs=(anywhere, anywhere, anywhere, vectors),
            scratch_shapes=[
                pltpu.VMEM((3, cx + 1, 2 * cy, depth), F32),
                pltpu.VMEM((STEPS + 1, 3, cx + 2, 2 * cy, depth), F32),
                pltpu.VMEM((3, cx + 1, 2 * cy, depth), F32),
                pltpu.VMEM((cx + 1, 2 * cy, depth), jnp.int32),
                pltpu.VMEM((cx + 1, 2 * cy, depth), jnp.int32),
                pltpu.VMEM((4, cx + 1, 2 * cy, depth), F32),
                pltpu.VMEM((STEPS, 4, cx, depth), F32),
                pltpu.VMEM((STEPS, 4, cx, depth), F32),
                pltpu.VMEM((STEPS, 4, 8, depth), F32),
                pltpu.VMEM((STEPS, 4, gy_count, depth), F32),
                pltpu.VMEM((8, 2, cx, freqs), F32),
                pltpu.VMEM((depth, 2 * freqs), F32),
                pltpu.VMEM((3, cx, dirs_x, freqs), F32),
                pltpu.VMEM((2, 2, dirs_x, freqs), F32),
                pltpu.VMEM((4, dirs_x, freqs), F32),
                pltpu.VMEM((4, gx_count, freqs), F32),
                pltpu.SemaphoreType.DMA((5,)),
                pltpu.SemaphoreType.DMA((STEPS, 14)),
                pltpu.SemaphoreType.DMA((STEPS, 14)),
                pltpu.SemaphoreType.DMA((STEPS, cx)),
                pltpu.SemaphoreType.DMA((STEPS, cx)),
                pltpu.SemaphoreType.DMA((STEPS, gy_count)),
                pltpu.SemaphoreType.DMA((STEPS, gy_count)),
                pltpu.SemaphoreType.DMA((gx_count,)),
                pltpu.SemaphoreType.DMA((gx_count,)),
            ],
            compiler_params=pltpu.CompilerParams(collective_id=0, has_side_effects=True),
        )(
            e_field,
            h_field,
            current,
            material,
            pole,
            permittivity,
            conductivity,
            plasma,
            damping,
            box,
            ux_index,
            uz_index,
            spectral_slot.reshape(1, freqs),
        )
        return e_field, h_field, current, far.reshape(4, 1, 1, freqs)

    fields = P(None, "gx", "gy", None)
    cells = P("gx", "gy", None)
    return jax.shard_map(
        body,
        mesh=mesh,
        in_specs=(fields, fields, fields, cells, cells) + (P(),) * 8,
        out_specs=(fields,) * 4,
        check_vma=False,
    )
```

```python
import math

import jax
import jax.numpy as jnp
from jax import lax
from jax.experimental import pallas as pl
from jax.experimental.pallas import tpu as pltpu
from jax.sharding import PartitionSpec as P

STEPS = 3
SPECTRUM_POINTS = 512
AGRID = 256
DT = 0.5
MESH = pl.DeviceIdType.MESH
F32 = jnp.float32
HIGHEST = lax.Precision.HIGHEST
TWO_OVER_PI = 0.6366197723675814
HALF_PI_HIGH = 1.5703125
HALF_PI_LOW = 4.838267948966e-4


def sincos(angle):
    turns = jnp.round(angle * TWO_OVER_PI)
    rest = (angle - turns * HALF_PI_HIGH) - turns * HALF_PI_LOW
    square = rest * rest
    sine = rest + rest * square * (
        -1.6666654611e-1 + square * (8.3321608736e-3 + square * -1.9515295891e-4)
    )
    cosine = (
        1.0
        - 0.5 * square
        + square
        * square
        * (4.166664568298827e-2 + square * (-1.388731625493765e-3 + square * 2.443315711809948e-5))
    )
    quadrant = turns.astype(jnp.int32)
    odd = (quadrant & 1) != 0
    sine_part = jnp.where(odd, cosine, sine)
    cosine_part = jnp.where(odd, sine, cosine)
    sine_out = jnp.where((quadrant & 2) != 0, -sine_part, sine_part)
    cosine_out = jnp.where(((quadrant + 1) & 2) != 0, -cosine_part, cosine_part)
    return cosine_out, sine_out


def write_out(*refs):
    sources, targets, sems = refs[0:4], refs[4:8], refs[8]
    copies = [
        pltpu.make_async_copy(source, target, sems.at[index])
        for index, (source, target) in enumerate(zip(sources, targets))
    ]
    for copy in copies:
        copy.start()
    for copy in copies:
        copy.wait()


def make_kernel(sizes):
    gx_count, gy_count, cx, cy, depth, freqs, dirs_x = sizes
    half = cx
    tiles = dirs_x // 8

    def kernel(
        e_in,
        h_in,
        j_in,
        m_in,
        p_in,
        permittivity,
        conductivity,
        plasma,
        damping,
        box,
        ux_index,
        uz_index,
        slot,
        e_out,
        h_out,
        j_out,
        far_out,
        E,
        H,
        J,
        M,
        Q,
        K,
        S,
        R,
        C,
        G,
        A,
        TZ,
        TX,
        TY,
        PART,
        RX,
        local_sem,
        halo_send,
        halo_recv,
        rs_send,
        rs_recv,
        ag_send,
        ag_recv,
        gx_send,
        gx_recv,
        row_sem,
    ):
        gx = lax.axis_index("gx")
        gy = lax.axis_index("gy")
        left = lax.rem(gx + gx_count - 1, gx_count)
        right = lax.rem(gx + 1, gx_count)
        below = lax.rem(gy + gy_count - 1, gy_count)
        above = lax.rem(gy + 1, gy_count)
        side = lax.div(gy, half)
        member = lax.rem(gy, half)

        own = (slice(None), pl.ds(0, cx), pl.ds(0, cy))
        local = [
            pltpu.make_async_copy(e_in, E.at[:, 0:cx, 0:cy, :], local_sem.at[0]),
            pltpu.make_async_copy(h_in, H.at[0, :, 0:cx, 0:cy, :], local_sem.at[1]),
            pltpu.make_async_copy(j_in, J.at[:, 0:cx, 0:cy, :], local_sem.at[2]),
            pltpu.make_async_copy(m_in, M.at[0:cx, 0:cy, :], local_sem.at[3]),
            pltpu.make_async_copy(p_in, Q.at[0:cx, 0:cy, :], local_sem.at[4]),
        ]
        for copy in local:
            copy.start()

        barrier = pltpu.get_barrier_semaphore()
        for place in ((left, gy), (right, gy), (left, above), (right, below)):
            pl.semaphore_signal(barrier, inc=1, device_id=place, device_id_type=MESH)

        def greet_column(step, carry):
            place = (gx, lax.rem(gy + step, gy_count))
            pl.semaphore_signal(barrier, inc=1, device_id=place, device_id_type=MESH)
            return carry

        lax.fori_loop(1, gy_count, greet_column, 0)

        for copy in local:
            copy.wait()
        pl.semaphore_wait(barrier, 4 + gy_count - 1)

        def halo(level):
            field = H.at[level]
            routes = [
                (field.at[:, 0, 0:cy, :], field.at[:, cx, 0:cy, :], (left, gy)),
                (field.at[1:3, cx - 1, 0:cy, :], field.at[1:3, cx + 1, 0:cy, :], (right, gy)),
                (field.at[:, 0:cx, 0, :], field.at[:, 0:cx, cy, :], (gx, below)),
                (field.at[:, 0:cx, cy - 1, :], field.at[:, 0:cx, 2 * cy - 1, :], (gx, above)),
                (field.at[0, 0, cy - 1, :], field.at[0, cx, 2 * cy - 1, :], (left, above)),
                (field.at[1, cx - 1, 0, :], field.at[1, cx + 1, cy, :], (right, below)),
            ]
            if level == 0:
                for ref in (E, J):
                    routes.append((ref.at[1:3, 0, 0:cy, :], ref.at[1:3, cx, 0:cy, :], (left, gy)))
                    routes.append((ref.at[:, 0:cx, 0, :], ref.at[:, 0:cx, cy, :], (gx, below)))
                for ref in (M, Q):
                    routes.append((ref.at[0, 0:cy, :], ref.at[cx, 0:cy, :], (left, gy)))
                    routes.append((ref.at[0:cx, 0, :], ref.at[0:cx, cy, :], (gx, below)))
            copies = []
            for index, (source, target, place) in enumerate(routes):
                copy = pltpu.make_async_remote_copy(
                    src_ref=source,
                    dst_ref=target,
                    send_sem=halo_send.at[level, index],
                    recv_sem=halo_recv.at[level, index],
                    device_id=place,
                    device_id_type=MESH,
                )
                copy.start()
                copies.append(copy)
            return copies

        pending = halo(0)

        omega = math.pi * (slot[...].astype(F32) + 0.5) / SPECTRUM_POINTS
        uz_own = -0.7 + 1.4 * (jnp.full((1, freqs), uz_index[gy], jnp.int32).astype(F32) + 0.5) / AGRID
        place_z = (lax.broadcasted_iota(jnp.int32, (depth, freqs), 0) - depth // 2).astype(F32)
        cos_z, sin_z = sincos((omega * uz_own) * place_z)
        TZ[:, 0:freqs] = cos_z
        TZ[:, freqs:] = sin_z

        sublane = lax.broadcasted_iota(jnp.int32, (8, freqs), 0)
        ux_tiles = []
        for tile in range(tiles):
            labels = jnp.zeros((8, freqs), jnp.int32)
            for row in range(8):
                labels = jnp.where(sublane == row, ux_index[tile * 8 + row], labels)
            ux_tiles.append(labels)
        ux = -0.7 + 1.4 * (jnp.concatenate(ux_tiles, axis=0).astype(F32) + 0.5) / AGRID
        omega_ux = omega * ux

        def fill_x(cell, carry):
            place_x = jnp.full((1, 1), gx * cx + cell - (gx_count * cx) // 2, jnp.int32).astype(F32)
            cos_x, sin_x = sincos(omega_ux * place_x)
            TX[0, cell] = cos_x
            TX[1, cell] = sin_x
            return carry

        lax.fori_loop(0, cx, fill_x, 0)
        uy = jnp.sqrt(1.0 - ux**2 - uz_own**2)
        for face in range(2):
            place_y = jnp.full((1, 1), box[2 + face] - (gy_count * cy) // 2, jnp.int32).astype(F32)
            cos_y, sin_y = sincos((omega * uy) * place_y)
            TY[face, 0] = cos_y
            TY[face, 1] = sin_y

        planes, rows = cx + 1, 2 * cy
        row = lax.broadcasted_iota(jnp.int32, (1, rows, depth), 1)
        lane = lax.broadcasted_iota(jnp.int32, (1, 1, depth), 2)
        first_row = (row == 0) & (gy == 0)
        outer_row = (row >= cy) & (gy == gy_count - 1)

        def prev_y(value):
            return jnp.where(first_row, 0.0, pltpu.roll(value, 1, 1))

        def prev_z(value):
            return jnp.where(lane == 0, 0.0, pltpu.roll(value, 1, 2))

        def next_z(value):
            return jnp.where(lane == depth - 1, 0.0, pltpu.roll(value, depth - 1, 2))

        table_row = lax.broadcasted_iota(jnp.int32, (8, depth), 0)

        def table(source, count):
            values = jnp.ones((8, depth), F32)
            for entry in range(count):
                values = jnp.where(table_row == entry, source[entry], values)
            return values

        eps_table = table(permittivity, 8)
        sig_table = table(conductivity, 8)
        plasma_table = table(plasma, 4)
        damping_table = table(damping, 4)
        loss = sig_table * DT / (2.0 * eps_table)
        keep_e_table = (1.0 - loss) / (1.0 + loss)
        drive_e_table = DT / eps_table / (1.0 + loss)
        rate = damping_table * DT / 2.0
        keep_j_table = (1.0 - rate) / (1.0 + rate)
        drive_j_table = plasma_table * DT / (1.0 + rate)

        y_row = lax.broadcasted_iota(jnp.int32, (1, cy, depth), 1) + gy * cy
        face_weight = jnp.where(y_row == box[3], 1.0, 0.0) - jnp.where(y_row == box[2], 1.0, 0.0)
        x_cell = lax.broadcasted_iota(jnp.int32, (cx, depth), 0) + gx * cx
        inside = jnp.where((x_cell >= box[0]) & (x_cell < box[1]), 1.0, 0.0)

        def scatter(step):
            copies = []
            for offset in range(1, half):
                other = lax.rem(member + offset, half)
                copy = pltpu.make_async_remote_copy(
                    src_ref=S.at[step, :, pl.ds(other, 1), :],
                    dst_ref=R.at[step, :, pl.ds(member, 1), :],
                    send_sem=rs_send.at[step, offset],
                    recv_sem=rs_recv.at[step, offset],
                    device_id=(gx, side * half + other),
                    device_id_type=MESH,
                )
                copy.start()
                copies.append(copy)
            R[step, :, pl.ds(member, 1), :] = S[step, :, pl.ds(member, 1), :]
            return copies

        def gather(step):
            total = jnp.sum(R[step], axis=1, keepdims=True)
            C[step, :, 0:1, :] = total
            copies = []
            for offset in sorted(range(1, gy_count), key=lambda value: abs(value - gy_count // 2)):
                other = lax.rem(gy + offset, gy_count)
                copy = pltpu.make_async_remote_copy(
                    src_ref=C.at[step, :, pl.ds(0, 1), :],
                    dst_ref=G.at[step, :, pl.ds(gy, 1), :],
                    send_sem=ag_send.at[step, offset],
                    recv_sem=ag_recv.at[step, offset],
                    device_id=(gx, other),
                    device_id_type=MESH,
                )
                copy.start()
                copies.append(copy)
            G[step, :, pl.ds(gy, 1), :] = total
            return copies

        greetings = []
        known = 2
        while known < gx_count // 2:
            greetings.append(known)
            known *= 2

        def greet(level):
            for shift in (greetings[level], gx_count - greetings[level]):
                pl.semaphore_signal(
                    row_sem.at[level],
                    inc=1,
                    device_id=(lax.rem(gx + shift, gx_count), gy),
                    device_id_type=MESH,
                )

        def greeted(level):
            pl.semaphore_wait(row_sem.at[level], 2)

        scatters = []
        gathers = []
        halos = []
        for step in range(STEPS):
            for copy in pending:
                copy.wait_recv()
            if step == 0:
                for copy in pending[6:10]:
                    copy.wait_send()
                halos.extend(pending[:6] + pending[10:])
            else:
                halos.extend(pending)
            if step == 0:
                material = M[...]
                pole = Q[...]
                plane = lax.broadcasted_iota(jnp.int32, (planes, rows, depth), 0)
                outside = outer_row | ((plane == cx) & (gx == gx_count - 1))
                keep_e = jnp.zeros((planes, rows, depth), F32)
                drive_e = jnp.zeros((planes, rows, depth), F32)
                for entry in range(8):
                    hit = material == entry
                    keep_e = jnp.where(hit, keep_e_table[entry : entry + 1, :][None], keep_e)
                    drive_e = jnp.where(hit, drive_e_table[entry : entry + 1, :][None], drive_e)
                keep_j = jnp.zeros((planes, rows, depth), F32)
                drive_j = jnp.zeros((planes, rows, depth), F32)
                for entry in range(4):
                    hit = pole == entry
                    keep_j = jnp.where(hit, keep_j_table[entry : entry + 1, :][None], keep_j)
                    drive_j = jnp.where(hit, drive_j_table[entry : entry + 1, :][None], drive_j)
                K[0] = jnp.where(outside, 0.0, keep_e)
                K[1] = jnp.where(outside, 0.0, drive_e)
                K[2] = keep_j
                K[3] = drive_j
            if step > 0:
                greeted(step - 1)
            greet(step)
            hx = H[step, 0, 0:planes]
            hy = H[step, 1, 0:planes]
            hz = H[step, 2, 0:planes]
            edge_y = jnp.where(gx == 0, 0.0, H[step, 1, planes : planes + 1])
            edge_z = jnp.where(gx == 0, 0.0, H[step, 2, planes : planes + 1])
            hy_x = jnp.concatenate([edge_y, hy[0 : planes - 1]], axis=0)
            hz_x = jnp.concatenate([edge_z, hz[0 : planes - 1]], axis=0)
            curls = (
                hz - prev_y(hz) - (hy - prev_z(hy)),
                hx - prev_z(hx) - (hz - hz_x),
                hy - hy_x - (hx - prev_y(hx)),
            )
            fresh = []
            for axis in range(3):
                old = E[axis]
                flow = K[2] * J[axis] + K[3] * old
                J[axis] = flow
                value = K[0] * old + K[1] * (curls[axis] - flow)
                E[axis] = value
                fresh.append(value)
            ex, ey, ez = fresh
            ex_o, ey_o, ez_o = (value[0:cx, 0:cy] for value in fresh)
            ex_y = pltpu.roll(ex, rows - 1, 1)[0:cx, 0:cy]
            ez_y = pltpu.roll(ez, rows - 1, 1)[0:cx, 0:cy]
            ey_x = ey[1 : cx + 1, 0:cy]
            ez_x = ez[1 : cx + 1, 0:cy]
            first = ez_y - ez_o - (next_z(ey_o) - ey_o)
            second = next_z(ex_o) - ex_o - (ez_x - ez_o)
            third = ey_x - ey_o - (ex_y - ex_o)
            new_h = []
            for axis, turn in enumerate((first, second, third)):
                value = H[step, axis, 0:cx, 0:cy] - DT * turn
                if step + 1 < STEPS:
                    H[step + 1, axis, 0:cx, 0:cy] = value
                else:
                    h_out[axis] = value
                    e_out[axis] = fresh[axis][0:cx, 0:cy]
                    j_out[axis] = J[axis, 0:cx, 0:cy]
                new_h.append(value)
            if step + 1 < STEPS:
                pending = halo(step + 1)
            for index, value in enumerate((new_h[2], -new_h[0], -ez_o, ex_o)):
                S[step, index] = jnp.sum(value * face_weight, axis=1) * inside
            scatters.append(scatter(step))
            if step > 0:
                for copy in scatters[step - 1]:
                    copy.wait_recv()
                gathers.append(gather(step - 1))
        for level in range(STEPS, len(greetings)):
            greeted(level - 1)
            greet(level)
        for copy in scatters[STEPS - 1]:
            copy.wait_recv()
        gathers.append(gather(STEPS - 1))

        real = [jnp.zeros((8, freqs), F32) for _ in range(8)]
        imag = [jnp.zeros((8, freqs), F32) for _ in range(8)]
        for step in range(STEPS):
            for copy in gathers[step]:
                copy.wait_recv()
            lines = jnp.dot(
                G[step].reshape(4 * gy_count, depth),
                TZ[...],
                precision=HIGHEST,
                preferred_element_type=F32,
            )
            cos_t, sin_t = sincos(omega * ((step + 1) * DT))
            for index in range(8):
                along_cos = lines[index * 8 : index * 8 + 8, 0:freqs]
                along_sin = lines[index * 8 : index * 8 + 8, freqs:]
                real[index] = real[index] + (along_cos * cos_t + along_sin * sin_t)
                imag[index] = imag[index] + (along_sin * cos_t - along_cos * sin_t)
        for index in range(8):
            A[index, 0] = real[index]
            A[index, 1] = imag[index]

        sine_theta = jnp.sqrt(1.0 - uz_own**2)
        scale = 1.0 / math.sqrt(gx_count * cx * depth)
        uz_over = uz_own / sine_theta
        inverse = 1.0 / sine_theta

        def project(tile, carry):
            start = pl.multiple_of(tile * 8, 8)
            span = pl.ds(start, 8)
            sums = []
            for index in range(8):
                total_re = jnp.zeros((8, freqs), F32)
                total_im = jnp.zeros((8, freqs), F32)
                for cell in range(cx):
                    a_re = A[index, 0, cell : cell + 1, :]
                    a_im = A[index, 1, cell : cell + 1, :]
                    c = TX[0, cell, span, :]
                    s = TX[1, cell, span, :]
                    total_re = total_re + (a_re * c - a_im * s)
                    total_im = total_im + (a_re * s + a_im * c)
                sums.append((total_re, total_im))
            turned = []
            for comp in range(4):
                out_re = jnp.zeros((8, freqs), F32)
                out_im = jnp.zeros((8, freqs), F32)
                for face in range(2):
                    value_re, value_im = sums[comp * 2 + face]
                    c = TY[face, 0, span, :]
                    s = TY[face, 1, span, :]
                    out_re = out_re + (value_re * c - value_im * s)
                    out_im = out_im + (value_re * s + value_im * c)
                turned.append((out_re * scale, out_im * scale))
            ux_here = TX[2, 0, span, :]
            uy_here = TX[2, 1, span, :]
            ratio_a = ux_here * uz_over
            ratio_b = uy_here * inverse
            for part in range(2):
                nx, nz, lx, lz = (turned[comp][part] for comp in range(4))
                PART[part, span, :] = lx * ratio_b - nx * ratio_a + nz * sine_theta
                PART[2 + part, span, :] = lx * ratio_a - lz * sine_theta + nx * ratio_b
            return carry

        TX[2, 0] = ux + jnp.zeros((dirs_x, freqs), F32)
        TX[2, 1] = uy
        lax.fori_loop(0, tiles, project, 0)

        def exchange(turn):
            away = lax.div(turn, 2)
            step = gx_count // 2 + jnp.where(lax.rem(turn, 2) == 0, away, -away)
            other = lax.rem(gx + step, gx_count)
            return pltpu.make_async_remote_copy(
                src_ref=PART.at[:, pl.ds(other, 1), :],
                dst_ref=RX.at[:, pl.ds(gx, 1), :],
                send_sem=gx_send.at[step],
                recv_sem=gx_recv.at[step],
                device_id=(other, gy),
                device_id_type=MESH,
            )

        def send(turn, carry):
            exchange(turn).start()
            return carry

        def receive(turn, carry):
            exchange(turn).wait_recv()
            return carry

        def finish(turn, carry):
            exchange(turn).wait_send()
            return carry

        greeted(len(greetings) - 1)
        lax.fori_loop(1, gx_count, send, 0)
        RX[:, pl.ds(gx, 1), :] = PART[:, pl.ds(gx, 1), :]
        for group in halos, *scatters, *gathers:
            for copy in group:
                copy.wait_send()
        lax.fori_loop(1, gx_count, receive, 0)
        far_out[...] = jnp.sum(RX[...], axis=1, keepdims=True)
        lax.fori_loop(1, gx_count, finish, 0)

    return kernel


def solution(mesh):
    gx_count = mesh.shape["gx"]
    gy_count = mesh.shape["gy"]

    def body(
        e_field,
        h_field,
        current,
        material,
        pole,
        permittivity,
        conductivity,
        plasma,
        damping,
        box,
        spectral_slot,
        ux_index,
        uz_index,
    ):
        _, cx, cy, depth = e_field.shape
        freqs = spectral_slot.shape[0]
        dirs_x = ux_index.shape[0]
        anywhere = pl.BlockSpec(memory_space=pl.ANY)
        scalars = pl.BlockSpec(memory_space=pltpu.SMEM)
        vectors = pl.BlockSpec(memory_space=pltpu.VMEM)
        inner = pltpu.VMEM(e_field.shape, F32)
        field = jax.ShapeDtypeStruct(e_field.shape, F32)
        e_field, h_field, current, far = pl.pallas_call(
            make_kernel((gx_count, gy_count, cx, cy, depth, freqs, dirs_x)),
            out_shape=(inner, inner, inner, pltpu.VMEM((4, 1, freqs), F32)),
            in_specs=[anywhere] * 5 + [scalars] * 7 + [vectors],
            out_specs=(vectors,) * 4,
            scratch_shapes=[
                pltpu.VMEM((3, cx + 1, 2 * cy, depth), F32),
                pltpu.VMEM((STEPS, 3, cx + 2, 2 * cy, depth), F32),
                pltpu.VMEM((3, cx + 1, 2 * cy, depth), F32),
                pltpu.VMEM((cx + 1, 2 * cy, depth), jnp.int32),
                pltpu.VMEM((cx + 1, 2 * cy, depth), jnp.int32),
                pltpu.VMEM((4, cx + 1, 2 * cy, depth), F32),
                pltpu.VMEM((STEPS, 4, cx, depth), F32),
                pltpu.VMEM((STEPS, 4, cx, depth), F32),
                pltpu.VMEM((STEPS, 4, 8, depth), F32),
                pltpu.VMEM((STEPS, 4, gy_count, depth), F32),
                pltpu.VMEM((8, 2, cx, freqs), F32),
                pltpu.VMEM((depth, 2 * freqs), F32),
                pltpu.VMEM((3, cx, dirs_x, freqs), F32),
                pltpu.VMEM((2, 2, dirs_x, freqs), F32),
                pltpu.VMEM((4, dirs_x, freqs), F32),
                pltpu.VMEM((4, gx_count, freqs), F32),
                pltpu.SemaphoreType.DMA((5,)),
                pltpu.SemaphoreType.DMA((STEPS, 14)),
                pltpu.SemaphoreType.DMA((STEPS, 14)),
                pltpu.SemaphoreType.DMA((STEPS, cx)),
                pltpu.SemaphoreType.DMA((STEPS, cx)),
                pltpu.SemaphoreType.DMA((STEPS, gy_count)),
                pltpu.SemaphoreType.DMA((STEPS, gy_count)),
                pltpu.SemaphoreType.DMA((gx_count,)),
                pltpu.SemaphoreType.DMA((gx_count,)),
                pltpu.SemaphoreType.REGULAR((8,)),
            ],
            compiler_params=pltpu.CompilerParams(collective_id=0, has_side_effects=True),
        )(
            e_field,
            h_field,
            current,
            material,
            pole,
            permittivity,
            conductivity,
            plasma,
            damping,
            box,
            ux_index,
            uz_index,
            spectral_slot.reshape(1, freqs),
        )
        e_field, h_field, current, far = pl.pallas_call(
            write_out,
            out_shape=(field, field, field, jax.ShapeDtypeStruct((4, 1, freqs), F32)),
            in_specs=[vectors] * 4,
            out_specs=(anywhere,) * 4,
            scratch_shapes=[pltpu.SemaphoreType.DMA((4,))],
        )(
            *(
                pltpu.with_memory_space_constraint(value, pltpu.VMEM)
                for value in (e_field, h_field, current, far)
            )
        )
        return e_field, h_field, current, far.reshape(4, 1, 1, freqs)

    fields = P(None, "gx", "gy", None)
    cells = P("gx", "gy", None)
    return jax.shard_map(
        body,
        mesh=mesh,
        in_specs=(fields, fields, fields, cells, cells) + (P(),) * 8,
        out_specs=(fields,) * 4,
        check_vma=False,
    )
```

```python
import math

import jax
import jax.numpy as jnp
from jax import lax
from jax.experimental import pallas as pl
from jax.experimental.pallas import tpu as pltpu
from jax.sharding import PartitionSpec as P

STEPS = 3
SPECTRUM_POINTS = 512
AGRID = 256
DT = 0.5
MESH = pl.DeviceIdType.MESH
F32 = jnp.float32
HIGHEST = lax.Precision.HIGHEST
TWO_OVER_PI = 0.6366197723675814
HALF_PI_HIGH = 1.5703125
HALF_PI_LOW = 4.838267948966e-4


def sincos(angle):
    turns = jnp.round(angle * TWO_OVER_PI)
    rest = (angle - turns * HALF_PI_HIGH) - turns * HALF_PI_LOW
    square = rest * rest
    sine = rest + rest * square * (
        -1.6666654611e-1 + square * (8.3321608736e-3 + square * -1.9515295891e-4)
    )
    cosine = (
        1.0
        - 0.5 * square
        + square
        * square
        * (4.166664568298827e-2 + square * (-1.388731625493765e-3 + square * 2.443315711809948e-5))
    )
    quadrant = turns.astype(jnp.int32)
    odd = (quadrant & 1) != 0
    sine_part = jnp.where(odd, cosine, sine)
    cosine_part = jnp.where(odd, sine, cosine)
    sine_out = jnp.where((quadrant & 2) != 0, -sine_part, sine_part)
    cosine_out = jnp.where(((quadrant + 1) & 2) != 0, -cosine_part, cosine_part)
    return cosine_out, sine_out


def write_out(*refs):
    sources, targets, sems = refs[0:4], refs[4:8], refs[8]
    copies = [
        pltpu.make_async_copy(source, target, sems.at[index])
        for index, (source, target) in enumerate(zip(sources, targets))
    ]
    for copy in copies:
        copy.start()
    for copy in copies:
        copy.wait()


def make_kernel(sizes):
    gx_count, gy_count, cx, cy, depth, freqs, dirs_x = sizes
    half = cx
    tiles = dirs_x // 8

    def kernel(
        e_in,
        h_in,
        j_in,
        m_in,
        p_in,
        permittivity_in,
        conductivity_in,
        plasma_in,
        damping_in,
        box_in,
        ux_in,
        uz_in,
        slot_in,
        e_out,
        h_out,
        j_out,
        far_out,
        E,
        H,
        J,
        M,
        Q,
        K,
        S,
        R,
        C,
        G,
        A,
        TZ,
        TX,
        TY,
        PART,
        RX,
        local_sem,
        halo_send,
        halo_recv,
        rs_send,
        rs_recv,
        ag_send,
        ag_recv,
        gx_send,
        gx_recv,
        row_sem,
        permittivity,
        conductivity,
        plasma,
        damping,
        box,
        ux_index,
        uz_index,
        slot,
    ):
        gx = lax.axis_index("gx")
        gy = lax.axis_index("gy")
        left = lax.rem(gx + gx_count - 1, gx_count)
        right = lax.rem(gx + 1, gx_count)
        below = lax.rem(gy + gy_count - 1, gy_count)
        above = lax.rem(gy + 1, gy_count)
        side = lax.div(gy, half)
        member = lax.rem(gy, half)

        own = (slice(None), pl.ds(0, cx), pl.ds(0, cy))
        barrier = pltpu.get_barrier_semaphore()
        for place in ((left, gy), (right, gy), (left, above), (right, below)):
            pl.semaphore_signal(barrier, inc=1, device_id=place, device_id_type=MESH)

        def greet_column(step, carry):
            place = (gx, lax.rem(gy + step, gy_count))
            pl.semaphore_signal(barrier, inc=1, device_id=place, device_id_type=MESH)
            return carry

        lax.fori_loop(1, gy_count, greet_column, 0)

        local = [
            pltpu.make_async_copy(e_in, E.at[:, 0:cx, 0:cy, :], local_sem.at[0]),
            pltpu.make_async_copy(h_in, H.at[0, :, 0:cx, 0:cy, :], local_sem.at[1]),
            pltpu.make_async_copy(j_in, J.at[:, 0:cx, 0:cy, :], local_sem.at[2]),
            pltpu.make_async_copy(m_in, M.at[0:cx, 0:cy, :], local_sem.at[3]),
            pltpu.make_async_copy(p_in, Q.at[0:cx, 0:cy, :], local_sem.at[4]),
        ]
        small = (permittivity_in, conductivity_in, plasma_in, damping_in, box_in, ux_in, uz_in)
        held = (permittivity, conductivity, plasma, damping, box, ux_index, uz_index)
        for index, (source, target) in enumerate(zip(small, held)):
            local.append(pltpu.make_async_copy(source, target, local_sem.at[5 + index]))
        local.append(pltpu.make_async_copy(slot_in, slot, local_sem.at[12]))
        for copy in local:
            copy.start()

        pl.semaphore_wait(barrier, 4 + gy_count - 1)

        def halo(level):
            field = H.at[level]
            held = h_in if level == 0 else field
            last_x, last_y = cx - 1, cy - 1
            routes = [
                (held.at[:, 0, 0:cy, :], field.at[:, cx, 0:cy, :], (left, gy)),
                (held.at[1:3, last_x, 0:cy, :], field.at[1:3, cx + 1, 0:cy, :], (right, gy)),
                (held.at[:, 0:cx, 0, :], field.at[:, 0:cx, cy, :], (gx, below)),
                (held.at[:, 0:cx, last_y, :], field.at[:, 0:cx, 2 * cy - 1, :], (gx, above)),
                (held.at[0, 0, last_y, :], field.at[0, cx, 2 * cy - 1, :], (left, above)),
                (held.at[1, last_x, 0, :], field.at[1, cx + 1, cy, :], (right, below)),
            ]
            if level == 0:
                for source, ref in ((e_in, E), (j_in, J)):
                    routes.append((source.at[1:3, 0, :, :], ref.at[1:3, cx, 0:cy, :], (left, gy)))
                    routes.append((source.at[:, :, 0, :], ref.at[:, 0:cx, cy, :], (gx, below)))
                for source, ref in ((m_in, M), (p_in, Q)):
                    routes.append((source.at[0, :, :], ref.at[cx, 0:cy, :], (left, gy)))
                    routes.append((source.at[:, 0, :], ref.at[0:cx, cy, :], (gx, below)))
            copies = []
            for index, (source, target, place) in enumerate(routes):
                copy = pltpu.make_async_remote_copy(
                    src_ref=source,
                    dst_ref=target,
                    send_sem=halo_send.at[level, index],
                    recv_sem=halo_recv.at[level, index],
                    device_id=place,
                    device_id_type=MESH,
                )
                copy.start()
                copies.append(copy)
            return copies

        pending = halo(0)
        for copy in local:
            copy.wait()

        omega = math.pi * (slot[...].astype(F32) + 0.5) / SPECTRUM_POINTS
        uz_own = -0.7 + 1.4 * (jnp.full((1, freqs), uz_index[gy], jnp.int32).astype(F32) + 0.5) / AGRID
        place_z = (lax.broadcasted_iota(jnp.int32, (depth, freqs), 0) - depth // 2).astype(F32)
        cos_z, sin_z = sincos((omega * uz_own) * place_z)
        TZ[:, 0:freqs] = cos_z
        TZ[:, freqs:] = sin_z

        sublane = lax.broadcasted_iota(jnp.int32, (8, freqs), 0)
        ux_tiles = []
        for tile in range(tiles):
            labels = jnp.zeros((8, freqs), jnp.int32)
            for row in range(8):
                labels = jnp.where(sublane == row, ux_index[tile * 8 + row], labels)
            ux_tiles.append(labels)
        ux = -0.7 + 1.4 * (jnp.concatenate(ux_tiles, axis=0).astype(F32) + 0.5) / AGRID
        omega_ux = omega * ux

        def fill_x(cell, carry):
            place_x = jnp.full((1, 1), gx * cx + cell - (gx_count * cx) // 2, jnp.int32).astype(F32)
            cos_x, sin_x = sincos(omega_ux * place_x)
            TX[0, cell] = cos_x
            TX[1, cell] = sin_x
            return carry

        lax.fori_loop(0, cx, fill_x, 0)
        uy = jnp.sqrt(1.0 - ux**2 - uz_own**2)
        for face in range(2):
            place_y = jnp.full((1, 1), box[2 + face] - (gy_count * cy) // 2, jnp.int32).astype(F32)
            cos_y, sin_y = sincos((omega * uy) * place_y)
            TY[face, 0] = cos_y
            TY[face, 1] = sin_y

        planes, rows = cx + 1, 2 * cy
        row = lax.broadcasted_iota(jnp.int32, (1, rows, depth), 1)
        lane = lax.broadcasted_iota(jnp.int32, (1, 1, depth), 2)
        first_row = (row == 0) & (gy == 0)
        outer_row = (row >= cy) & (gy == gy_count - 1)

        def prev_y(value):
            return jnp.where(first_row, 0.0, pltpu.roll(value, 1, 1))

        def prev_z(value):
            return jnp.where(lane == 0, 0.0, pltpu.roll(value, 1, 2))

        def next_z(value):
            return jnp.where(lane == depth - 1, 0.0, pltpu.roll(value, depth - 1, 2))

        table_row = lax.broadcasted_iota(jnp.int32, (8, depth), 0)

        def table(source, count):
            values = jnp.ones((8, depth), F32)
            for entry in range(count):
                values = jnp.where(table_row == entry, source[entry], values)
            return values

        eps_table = table(permittivity, 8)
        sig_table = table(conductivity, 8)
        plasma_table = table(plasma, 4)
        damping_table = table(damping, 4)
        loss = sig_table * DT / (2.0 * eps_table)
        keep_e_table = (1.0 - loss) / (1.0 + loss)
        drive_e_table = DT / eps_table / (1.0 + loss)
        rate = damping_table * DT / 2.0
        keep_j_table = (1.0 - rate) / (1.0 + rate)
        drive_j_table = plasma_table * DT / (1.0 + rate)

        y_row = lax.broadcasted_iota(jnp.int32, (1, cy, depth), 1) + gy * cy
        face_weight = jnp.where(y_row == box[3], 1.0, 0.0) - jnp.where(y_row == box[2], 1.0, 0.0)
        x_cell = lax.broadcasted_iota(jnp.int32, (cx, depth), 0) + gx * cx
        inside = jnp.where((x_cell >= box[0]) & (x_cell < box[1]), 1.0, 0.0)

        def scatter(step):
            copies = []
            for offset in range(1, half):
                other = lax.rem(member + offset, half)
                copy = pltpu.make_async_remote_copy(
                    src_ref=S.at[step, :, pl.ds(other, 1), :],
                    dst_ref=R.at[step, :, pl.ds(member, 1), :],
                    send_sem=rs_send.at[step, offset],
                    recv_sem=rs_recv.at[step, offset],
                    device_id=(gx, side * half + other),
                    device_id_type=MESH,
                )
                copy.start()
                copies.append(copy)
            R[step, :, pl.ds(member, 1), :] = S[step, :, pl.ds(member, 1), :]
            return copies

        def gather(step):
            total = jnp.sum(R[step], axis=1, keepdims=True)
            C[step, :, 0:1, :] = total
            copies = []
            for offset in sorted(range(1, gy_count), key=lambda value: abs(value - gy_count // 2)):
                other = lax.rem(gy + offset, gy_count)
                copy = pltpu.make_async_remote_copy(
                    src_ref=C.at[step, :, pl.ds(0, 1), :],
                    dst_ref=G.at[step, :, pl.ds(gy, 1), :],
                    send_sem=ag_send.at[step, offset],
                    recv_sem=ag_recv.at[step, offset],
                    device_id=(gx, other),
                    device_id_type=MESH,
                )
                copy.start()
                copies.append(copy)
            G[step, :, pl.ds(gy, 1), :] = total
            return copies

        greetings = []
        known = 2
        while known < gx_count // 2:
            greetings.append(known)
            known *= 2

        def greet(level):
            for shift in (greetings[level], gx_count - greetings[level]):
                pl.semaphore_signal(
                    row_sem.at[level],
                    inc=1,
                    device_id=(lax.rem(gx + shift, gx_count), gy),
                    device_id_type=MESH,
                )

        def greeted(level):
            pl.semaphore_wait(row_sem.at[level], 2)

        scatters = []
        gathers = []
        halos = []
        for step in range(STEPS):
            for copy in pending:
                copy.wait_recv()
            halos.extend(pending)
            if step == 0:
                material = M[...]
                pole = Q[...]
                plane = lax.broadcasted_iota(jnp.int32, (planes, rows, depth), 0)
                outside = outer_row | ((plane == cx) & (gx == gx_count - 1))
                keep_e = jnp.zeros((planes, rows, depth), F32)
                drive_e = jnp.zeros((planes, rows, depth), F32)
                for entry in range(8):
                    hit = material == entry
                    keep_e = jnp.where(hit, keep_e_table[entry : entry + 1, :][None], keep_e)
                    drive_e = jnp.where(hit, drive_e_table[entry : entry + 1, :][None], drive_e)
                keep_j = jnp.zeros((planes, rows, depth), F32)
                drive_j = jnp.zeros((planes, rows, depth), F32)
                for entry in range(4):
                    hit = pole == entry
                    keep_j = jnp.where(hit, keep_j_table[entry : entry + 1, :][None], keep_j)
                    drive_j = jnp.where(hit, drive_j_table[entry : entry + 1, :][None], drive_j)
                K[0] = jnp.where(outside, 0.0, keep_e)
                K[1] = jnp.where(outside, 0.0, drive_e)
                K[2] = keep_j
                K[3] = drive_j
            if step > 0:
                greeted(step - 1)
            greet(step)
            hx = H[step, 0, 0:planes]
            hy = H[step, 1, 0:planes]
            hz = H[step, 2, 0:planes]
            edge_y = jnp.where(gx == 0, 0.0, H[step, 1, planes : planes + 1])
            edge_z = jnp.where(gx == 0, 0.0, H[step, 2, planes : planes + 1])
            hy_x = jnp.concatenate([edge_y, hy[0 : planes - 1]], axis=0)
            hz_x = jnp.concatenate([edge_z, hz[0 : planes - 1]], axis=0)
            curls = (
                hz - prev_y(hz) - (hy - prev_z(hy)),
                hx - prev_z(hx) - (hz - hz_x),
                hy - hy_x - (hx - prev_y(hx)),
            )
            fresh = []
            for axis in range(3):
                old = E[axis]
                flow = K[2] * J[axis] + K[3] * old
                J[axis] = flow
                value = K[0] * old + K[1] * (curls[axis] - flow)
                E[axis] = value
                fresh.append(value)
            ex, ey, ez = fresh
            ex_o, ey_o, ez_o = (value[0:cx, 0:cy] for value in fresh)
            ex_y = pltpu.roll(ex, rows - 1, 1)[0:cx, 0:cy]
            ez_y = pltpu.roll(ez, rows - 1, 1)[0:cx, 0:cy]
            ey_x = ey[1 : cx + 1, 0:cy]
            ez_x = ez[1 : cx + 1, 0:cy]
            first = ez_y - ez_o - (next_z(ey_o) - ey_o)
            second = next_z(ex_o) - ex_o - (ez_x - ez_o)
            third = ey_x - ey_o - (ex_y - ex_o)
            new_h = []
            for axis, turn in enumerate((first, second, third)):
                value = H[step, axis, 0:cx, 0:cy] - DT * turn
                if step + 1 < STEPS:
                    H[step + 1, axis, 0:cx, 0:cy] = value
                else:
                    h_out[axis] = value
                    e_out[axis] = fresh[axis][0:cx, 0:cy]
                    j_out[axis] = J[axis, 0:cx, 0:cy]
                new_h.append(value)
            if step + 1 < STEPS:
                pending = halo(step + 1)
            for index, value in enumerate((new_h[2], -new_h[0], -ez_o, ex_o)):
                S[step, index] = jnp.sum(value * face_weight, axis=1) * inside
            scatters.append(scatter(step))
            if step > 0:
                for copy in scatters[step - 1]:
                    copy.wait_recv()
                gathers.append(gather(step - 1))
        for level in range(STEPS, len(greetings)):
            greeted(level - 1)
            greet(level)
        for copy in scatters[STEPS - 1]:
            copy.wait_recv()
        gathers.append(gather(STEPS - 1))

        real = [jnp.zeros((8, freqs), F32) for _ in range(8)]
        imag = [jnp.zeros((8, freqs), F32) for _ in range(8)]
        for step in range(STEPS):
            for copy in gathers[step]:
                copy.wait_recv()
            lines = jnp.dot(
                G[step].reshape(4 * gy_count, depth),
                TZ[...],
                precision=HIGHEST,
                preferred_element_type=F32,
            )
            cos_t, sin_t = sincos(omega * ((step + 1) * DT))
            for index in range(8):
                along_cos = lines[index * 8 : index * 8 + 8, 0:freqs]
                along_sin = lines[index * 8 : index * 8 + 8, freqs:]
                real[index] = real[index] + (along_cos * cos_t + along_sin * sin_t)
                imag[index] = imag[index] + (along_sin * cos_t - along_cos * sin_t)
        for index in range(8):
            A[index, 0] = real[index]
            A[index, 1] = imag[index]

        sine_theta = jnp.sqrt(1.0 - uz_own**2)
        scale = 1.0 / math.sqrt(gx_count * cx * depth)
        uz_over = uz_own / sine_theta
        inverse = 1.0 / sine_theta

        def project(tile):
            start = pl.multiple_of(tile * 8, 8)
            span = pl.ds(start, 8)
            sums = []
            for index in range(8):
                total_re = jnp.zeros((8, freqs), F32)
                total_im = jnp.zeros((8, freqs), F32)
                for cell in range(cx):
                    a_re = A[index, 0, cell : cell + 1, :]
                    a_im = A[index, 1, cell : cell + 1, :]
                    c = TX[0, cell, span, :]
                    s = TX[1, cell, span, :]
                    total_re = total_re + (a_re * c - a_im * s)
                    total_im = total_im + (a_re * s + a_im * c)
                sums.append((total_re, total_im))
            turned = []
            for comp in range(4):
                out_re = jnp.zeros((8, freqs), F32)
                out_im = jnp.zeros((8, freqs), F32)
                for face in range(2):
                    value_re, value_im = sums[comp * 2 + face]
                    c = TY[face, 0, span, :]
                    s = TY[face, 1, span, :]
                    out_re = out_re + (value_re * c - value_im * s)
                    out_im = out_im + (value_re * s + value_im * c)
                turned.append((out_re * scale, out_im * scale))
            ux_here = TX[2, 0, span, :]
            uy_here = TX[2, 1, span, :]
            ratio_a = ux_here * uz_over
            ratio_b = uy_here * inverse
            for part in range(2):
                nx, nz, lx, lz = (turned[comp][part] for comp in range(4))
                PART[part, span, :] = lx * ratio_b - nx * ratio_a + nz * sine_theta
                PART[2 + part, span, :] = lx * ratio_a - lz * sine_theta + nx * ratio_b

        TX[2, 0] = ux + jnp.zeros((dirs_x, freqs), F32)
        TX[2, 1] = uy

        def exchange(other):
            step = lax.rem(other + gx_count - gx, gx_count)
            return pltpu.make_async_remote_copy(
                src_ref=PART.at[:, pl.ds(other, 1), :],
                dst_ref=RX.at[:, pl.ds(gx, 1), :],
                send_sem=gx_send.at[step],
                recv_sem=gx_recv.at[step],
                device_id=(other, gy),
                device_id_type=MESH,
            )

        def send(other, carry):
            @pl.when(other != gx)
            def _():
                exchange(other).start()

            return carry

        def project_and_send(turn, carry):
            away = lax.div(turn + 1, 2)
            away = jnp.where(lax.rem(turn, 2) == 0, away, -away)
            tile = lax.rem(lax.div(gx, 8) + tiles // 2 + away + tiles, tiles)
            project(tile)
            lax.fori_loop(tile * 8, tile * 8 + 8, send, 0)
            return carry

        def receive(step, carry):
            exchange(lax.rem(gx + step, gx_count)).wait_recv()
            return carry

        def finish(step, carry):
            exchange(lax.rem(gx + step, gx_count)).wait_send()
            return carry

        greeted(len(greetings) - 1)
        lax.fori_loop(0, tiles, project_and_send, 0)
        RX[:, pl.ds(gx, 1), :] = PART[:, pl.ds(gx, 1), :]
        for group in halos, *scatters, *gathers:
            for copy in group:
                copy.wait_send()
        lax.fori_loop(1, gx_count, receive, 0)
        far_out[...] = jnp.sum(RX[...], axis=1, keepdims=True)
        lax.fori_loop(1, gx_count, finish, 0)

    return kernel


def solution(mesh):
    gx_count = mesh.shape["gx"]
    gy_count = mesh.shape["gy"]

    def body(
        e_field,
        h_field,
        current,
        material,
        pole,
        permittivity,
        conductivity,
        plasma,
        damping,
        box,
        spectral_slot,
        ux_index,
        uz_index,
    ):
        _, cx, cy, depth = e_field.shape
        freqs = spectral_slot.shape[0]
        dirs_x = ux_index.shape[0]
        anywhere = pl.BlockSpec(memory_space=pl.ANY)
        vectors = pl.BlockSpec(memory_space=pltpu.VMEM)
        inner = pltpu.VMEM(e_field.shape, F32)
        field = jax.ShapeDtypeStruct(e_field.shape, F32)
        e_field, h_field, current, far = pl.pallas_call(
            make_kernel((gx_count, gy_count, cx, cy, depth, freqs, dirs_x)),
            out_shape=(inner, inner, inner, pltpu.VMEM((4, 1, freqs), F32)),
            in_specs=[anywhere] * 13,
            out_specs=(vectors,) * 4,
            scratch_shapes=[
                pltpu.VMEM((3, cx + 1, 2 * cy, depth), F32),
                pltpu.VMEM((STEPS, 3, cx + 2, 2 * cy, depth), F32),
                pltpu.VMEM((3, cx + 1, 2 * cy, depth), F32),
                pltpu.VMEM((cx + 1, 2 * cy, depth), jnp.int32),
                pltpu.VMEM((cx + 1, 2 * cy, depth), jnp.int32),
                pltpu.VMEM((4, cx + 1, 2 * cy, depth), F32),
                pltpu.VMEM((STEPS, 4, cx, depth), F32),
                pltpu.VMEM((STEPS, 4, cx, depth), F32),
                pltpu.VMEM((STEPS, 4, 8, depth), F32),
                pltpu.VMEM((STEPS, 4, gy_count, depth), F32),
                pltpu.VMEM((8, 2, cx, freqs), F32),
                pltpu.VMEM((depth, 2 * freqs), F32),
                pltpu.VMEM((3, cx, dirs_x, freqs), F32),
                pltpu.VMEM((2, 2, dirs_x, freqs), F32),
                pltpu.VMEM((4, dirs_x, freqs), F32),
                pltpu.VMEM((4, gx_count, freqs), F32),
                pltpu.SemaphoreType.DMA((13,)),
                pltpu.SemaphoreType.DMA((STEPS, 14)),
                pltpu.SemaphoreType.DMA((STEPS, 14)),
                pltpu.SemaphoreType.DMA((STEPS, cx)),
                pltpu.SemaphoreType.DMA((STEPS, cx)),
                pltpu.SemaphoreType.DMA((STEPS, gy_count)),
                pltpu.SemaphoreType.DMA((STEPS, gy_count)),
                pltpu.SemaphoreType.DMA((gx_count,)),
                pltpu.SemaphoreType.DMA((gx_count,)),
                pltpu.SemaphoreType.REGULAR((8,)),
                pltpu.SMEM(permittivity.shape, F32),
                pltpu.SMEM(conductivity.shape, F32),
                pltpu.SMEM(plasma.shape, F32),
                pltpu.SMEM(damping.shape, F32),
                pltpu.SMEM(box.shape, jnp.int32),
                pltpu.SMEM(ux_index.shape, jnp.int32),
                pltpu.SMEM(uz_index.shape, jnp.int32),
                pltpu.VMEM((1, freqs), jnp.int32),
            ],
            compiler_params=pltpu.CompilerParams(collective_id=0, has_side_effects=True),
        )(
            e_field,
            h_field,
            current,
            material,
            pole,
            permittivity,
            conductivity,
            plasma,
            damping,
            box,
            ux_index,
            uz_index,
            spectral_slot.reshape(1, freqs),
        )
        e_field, h_field, current, far = pl.pallas_call(
            write_out,
            out_shape=(field, field, field, jax.ShapeDtypeStruct((4, 1, freqs), F32)),
            in_specs=[vectors] * 4,
            out_specs=(anywhere,) * 4,
            scratch_shapes=[pltpu.SemaphoreType.DMA((4,))],
        )(
            *(
                pltpu.with_memory_space_constraint(value, pltpu.VMEM)
                for value in (e_field, h_field, current, far)
            )
        )
        return e_field, h_field, current, far.reshape(4, 1, 1, freqs)

    fields = P(None, "gx", "gy", None)
    cells = P("gx", "gy", None)
    return jax.shard_map(
        body,
        mesh=mesh,
        in_specs=(fields, fields, fields, cells, cells) + (P(),) * 8,
        out_specs=(fields,) * 4,
        check_vma=False,
    )
```

```python
import math

import jax
import jax.numpy as jnp
from jax import lax
from jax.experimental import pallas as pl
from jax.experimental.pallas import tpu as pltpu
from jax.sharding import PartitionSpec as P

STEPS = 3
SPECTRUM_POINTS = 512
AGRID = 256
LOW_FIRST, LOW_LAST = 1, 32
HIGH_FIRST, HIGH_LAST = 96, 127
DT = 0.5
MESH = pl.DeviceIdType.MESH
F32 = jnp.float32
HIGHEST = lax.Precision.HIGHEST
TWO_OVER_PI = 0.6366197723675814
HALF_PI_HIGH = 1.5703125
HALF_PI_LOW = 4.838267948966e-4


def sincos(angle):
    turns = jnp.round(angle * TWO_OVER_PI)
    rest = (angle - turns * HALF_PI_HIGH) - turns * HALF_PI_LOW
    square = rest * rest
    sine = rest + rest * square * (
        -1.6666654611e-1 + square * (8.3321608736e-3 + square * -1.9515295891e-4)
    )
    cosine = (
        1.0
        - 0.5 * square
        + square
        * square
        * (4.166664568298827e-2 + square * (-1.388731625493765e-3 + square * 2.443315711809948e-5))
    )
    quadrant = turns.astype(jnp.int32)
    odd = (quadrant & 1) != 0
    sine_part = jnp.where(odd, cosine, sine)
    cosine_part = jnp.where(odd, sine, cosine)
    sine_out = jnp.where((quadrant & 2) != 0, -sine_part, sine_part)
    cosine_out = jnp.where(((quadrant + 1) & 2) != 0, -cosine_part, cosine_part)
    return cosine_out, sine_out


def write_out(*refs):
    sources, targets, sems = refs[0:4], refs[4:8], refs[8]
    copies = [
        pltpu.make_async_copy(source, target, sems.at[index])
        for index, (source, target) in enumerate(zip(sources, targets))
    ]
    for copy in copies:
        copy.start()
    for copy in copies:
        copy.wait()


def make_kernel(sizes):
    gx_count, gy_count, cx, cy, depth, freqs, dirs_x = sizes
    owners = 4
    share = cx // owners
    tiles = dirs_x // 8

    def kernel(
        e_in,
        h_in,
        j_in,
        m_in,
        p_in,
        permittivity_in,
        conductivity_in,
        plasma_in,
        damping_in,
        box_in,
        ux_in,
        uz_in,
        slot_in,
        e_out,
        h_out,
        j_out,
        far_out,
        E,
        H,
        J,
        M,
        Q,
        K,
        S,
        R,
        C,
        G,
        A,
        TZ,
        TX,
        TY,
        PART,
        RX,
        local_sem,
        halo_send,
        halo_recv,
        rs_send,
        rs_recv,
        ag_send,
        ag_recv,
        gx_send,
        gx_recv,
        row_sem,
        permittivity,
        conductivity,
        plasma,
        damping,
        box,
        ux_index,
        uz_index,
        slot,
    ):
        gx = lax.axis_index("gx")
        gy = lax.axis_index("gy")
        left = lax.rem(gx + gx_count - 1, gx_count)
        right = lax.rem(gx + 1, gx_count)
        below = lax.rem(gy + gy_count - 1, gy_count)
        above = lax.rem(gy + 1, gy_count)

        own = (slice(None), pl.ds(0, cx), pl.ds(0, cy))
        barrier = pltpu.get_barrier_semaphore()
        for place in ((left, above), (right, below)):
            pl.semaphore_signal(barrier, inc=1, device_id=place, device_id_type=MESH)

        def greet_column(step, carry):
            place = (gx, lax.rem(gy + step, gy_count))
            pl.semaphore_signal(barrier, inc=1, device_id=place, device_id_type=MESH)
            return carry

        def greet_row(shift, carry):
            for place in (gx + shift, gx + gx_count - shift):
                pl.semaphore_signal(
                    barrier,
                    inc=1,
                    device_id=(lax.rem(place, gx_count), gy),
                    device_id_type=MESH,
                )
            return carry

        near = (gx_count // 2 + 1) // 2
        lax.fori_loop(1, near + 1, greet_row, 0)
        lax.fori_loop(1, gy_count, greet_column, 0)

        local = [
            pltpu.make_async_copy(e_in, E.at[:, 0:cx, 0:cy, :], local_sem.at[0]),
            pltpu.make_async_copy(h_in, H.at[0, :, 0:cx, 0:cy, :], local_sem.at[1]),
            pltpu.make_async_copy(j_in, J.at[:, 0:cx, 0:cy, :], local_sem.at[2]),
            pltpu.make_async_copy(m_in, M.at[0:cx, 0:cy, :], local_sem.at[3]),
            pltpu.make_async_copy(p_in, Q.at[0:cx, 0:cy, :], local_sem.at[4]),
        ]
        small = (permittivity_in, conductivity_in, plasma_in, damping_in, box_in, ux_in, uz_in)
        held = (permittivity, conductivity, plasma, damping, box, ux_index, uz_index)
        for index, (source, target) in enumerate(zip(small, held)):
            local.append(pltpu.make_async_copy(source, target, local_sem.at[5 + index]))
        local.append(pltpu.make_async_copy(slot_in, slot, local_sem.at[12]))
        for copy in local:
            copy.start()

        pl.semaphore_wait(barrier, 2 + 2 * near + gy_count - 1)
        for place in (gx + near, gx + gx_count - near):
            pl.semaphore_signal(
                row_sem.at[0],
                inc=1,
                device_id=(lax.rem(place, gx_count), gy),
                device_id_type=MESH,
            )

        def halo(level):
            field = H.at[level]
            held = h_in if level == 0 else field
            last_x, last_y = cx - 1, cy - 1
            routes = [
                (held.at[:, 0, 0:cy, :], field.at[:, cx, 0:cy, :], (left, gy)),
                (held.at[1:3, last_x, 0:cy, :], field.at[1:3, cx + 1, 0:cy, :], (right, gy)),
                (held.at[:, 0:cx, 0, :], field.at[:, 0:cx, cy, :], (gx, below)),
                (held.at[:, 0:cx, last_y, :], field.at[:, 0:cx, 2 * cy - 1, :], (gx, above)),
                (held.at[0, 0, last_y, :], field.at[0, cx, 2 * cy - 1, :], (left, above)),
                (held.at[1, last_x, 0, :], field.at[1, cx + 1, cy, :], (right, below)),
            ]
            if level == 0:
                for source, ref in ((e_in, E), (j_in, J)):
                    routes.append((source.at[1:3, 0, :, :], ref.at[1:3, cx, 0:cy, :], (left, gy)))
                    routes.append((source.at[:, :, 0, :], ref.at[:, 0:cx, cy, :], (gx, below)))
                for source, ref in ((m_in, M), (p_in, Q)):
                    routes.append((source.at[0, :, :], ref.at[cx, 0:cy, :], (left, gy)))
                    routes.append((source.at[:, 0, :], ref.at[0:cx, cy, :], (gx, below)))
            copies = []
            for index, (source, target, place) in enumerate(routes):
                copy = pltpu.make_async_remote_copy(
                    src_ref=source,
                    dst_ref=target,
                    send_sem=halo_send.at[level, index],
                    recv_sem=halo_recv.at[level, index],
                    device_id=place,
                    device_id_type=MESH,
                )
                copy.start()
                copies.append(copy)
            return copies

        pending = halo(0)
        for copy in local:
            copy.wait()

        omega = math.pi * (slot[...].astype(F32) + 0.5) / SPECTRUM_POINTS
        uz_own = -0.7 + 1.4 * (jnp.full((1, freqs), uz_index[gy], jnp.int32).astype(F32) + 0.5) / AGRID
        place_z = (lax.broadcasted_iota(jnp.int32, (depth, freqs), 0) - depth // 2).astype(F32)
        cos_z, sin_z = sincos((omega * uz_own) * place_z)
        TZ[:, 0:freqs] = cos_z
        TZ[:, freqs:] = sin_z

        sublane = lax.broadcasted_iota(jnp.int32, (8, freqs), 0)
        ux_tiles = []
        for tile in range(tiles):
            labels = jnp.zeros((8, freqs), jnp.int32)
            for row in range(8):
                labels = jnp.where(sublane == row, ux_index[tile * 8 + row], labels)
            ux_tiles.append(labels)
        ux = -0.7 + 1.4 * (jnp.concatenate(ux_tiles, axis=0).astype(F32) + 0.5) / AGRID
        omega_ux = omega * ux

        def fill_x(cell, carry):
            place_x = jnp.full((1, 1), gx * cx + cell - (gx_count * cx) // 2, jnp.int32).astype(F32)
            cos_x, sin_x = sincos(omega_ux * place_x)
            TX[0, cell] = cos_x
            TX[1, cell] = sin_x
            return carry

        lax.fori_loop(0, cx, fill_x, 0)
        uy = jnp.sqrt(1.0 - ux**2 - uz_own**2)
        for face in range(2):
            place_y = jnp.full((1, 1), box[2 + face] - (gy_count * cy) // 2, jnp.int32).astype(F32)
            cos_y, sin_y = sincos((omega * uy) * place_y)
            TY[face, 0] = cos_y
            TY[face, 1] = sin_y

        planes, rows = cx + 1, 2 * cy
        row = lax.broadcasted_iota(jnp.int32, (1, rows, depth), 1)
        lane = lax.broadcasted_iota(jnp.int32, (1, 1, depth), 2)
        first_row = (row == 0) & (gy == 0)
        outer_row = (row >= cy) & (gy == gy_count - 1)

        def prev_y(value):
            return jnp.where(first_row, 0.0, pltpu.roll(value, 1, 1))

        def prev_z(value):
            return jnp.where(lane == 0, 0.0, pltpu.roll(value, 1, 2))

        def next_z(value):
            return jnp.where(lane == depth - 1, 0.0, pltpu.roll(value, depth - 1, 2))

        table_row = lax.broadcasted_iota(jnp.int32, (8, depth), 0)

        def table(source, count):
            values = jnp.ones((8, depth), F32)
            for entry in range(count):
                values = jnp.where(table_row == entry, source[entry], values)
            return values

        eps_table = table(permittivity, 8)
        sig_table = table(conductivity, 8)
        plasma_table = table(plasma, 4)
        damping_table = table(damping, 4)
        loss = sig_table * DT / (2.0 * eps_table)
        keep_e_table = (1.0 - loss) / (1.0 + loss)
        drive_e_table = DT / eps_table / (1.0 + loss)
        rate = damping_table * DT / 2.0
        keep_j_table = (1.0 - rate) / (1.0 + rate)
        drive_j_table = plasma_table * DT / (1.0 + rate)

        y_row = lax.broadcasted_iota(jnp.int32, (1, cy, depth), 1) + gy * cy
        face_weight = jnp.where(y_row == box[3], 1.0, 0.0) - jnp.where(y_row == box[2], 1.0, 0.0)
        x_cell = lax.broadcasted_iota(jnp.int32, (cx, depth), 0) + gx * cx
        inside = jnp.where((x_cell >= box[0]) & (x_cell < box[1]), 1.0, 0.0)

        low = gy < gy_count // 2
        base = jnp.where(low, LOW_FIRST // cy, HIGH_FIRST // cy)
        place = gy - base
        members = jnp.where(low, LOW_LAST // cy, HIGH_LAST // cy) - base + 1
        holds = (place >= 0) & (place < members)
        collects = (place >= 0) & (place < owners)
        quarter = jnp.where(low, 0, owners) + place
        slots = 1 + max(LOW_LAST // cy - LOW_FIRST // cy, HIGH_LAST // cy - HIGH_FIRST // cy)

        def to_owner(step, owner):
            cells = pl.ds(owner * share, share)
            return pltpu.make_async_remote_copy(
                src_ref=S.at[step, :, cells, :],
                dst_ref=R.at[step, place, :, cells, :],
                send_sem=rs_send.at[step, owner],
                recv_sem=rs_recv.at[step, place],
                device_id=(gx, base + owner),
                device_id_type=MESH,
            )

        def from_member(step, member):
            cells = pl.ds(place * share, share)
            return pltpu.make_async_remote_copy(
                src_ref=S.at[step, :, cells, :],
                dst_ref=R.at[step, member, :, cells, :],
                send_sem=rs_send.at[step, 0],
                recv_sem=rs_recv.at[step, member],
                device_id=(gx, base + member),
                device_id_type=MESH,
            )

        def to_column(step, offset):
            return pltpu.make_async_remote_copy(
                src_ref=C.at[step, :, pl.ds(place * share, share), :],
                dst_ref=G.at[step, :, pl.ds(quarter * share, share), :],
                send_sem=ag_send.at[step, offset],
                recv_sem=ag_recv.at[step, quarter],
                device_id=(gx, lax.rem(gy + offset, gy_count)),
                device_id_type=MESH,
            )

        def from_column(step, part):
            cells = pl.ds(part * share, share)
            return pltpu.make_async_remote_copy(
                src_ref=G.at[step, :, cells, :],
                dst_ref=G.at[step, :, cells, :],
                send_sem=ag_send.at[step, 0],
                recv_sem=ag_recv.at[step, part],
                device_id=(gx, above),
                device_id_type=MESH,
            )

        def scatter(step):
            for owner in range(owners):

                @pl.when(holds & (place != owner))
                def _():
                    to_owner(step, owner).start()

            @pl.when(collects)
            def _():
                R[step, place] = S[step]

        def gather(step):
            @pl.when(collects)
            def _():
                for member in range(slots):

                    @pl.when((place != member) & (member < members))
                    def _():
                        from_member(step, member).wait_recv()

                total = R[step, 0]
                for member in range(1, slots):
                    total = total + jnp.where(member < members, R[step, member], 0.0)
                C[step] = total
                for offset in sorted(range(1, gy_count), key=lambda value: abs(value - gy_count // 2)):
                    to_column(step, offset).start()
                for cell in range(share):
                    G[step, :, pl.ds(quarter * share + cell, 1), :] = C[
                        step, :, pl.ds(place * share + cell, 1), :
                    ]

        def gathered(step):
            for part in range(2 * owners):
                owner = part if part < owners else HIGH_FIRST // cy + part - owners

                @pl.when(gy != owner)
                def _():
                    from_column(step, part).wait_recv()

        def collected(step):
            for owner in range(owners):

                @pl.when(holds & (place != owner))
                def _():
                    to_owner(step, owner).wait_send()

            @pl.when(collects)
            def _():
                for offset in range(1, gy_count):
                    to_column(step, offset).wait_send()

        halos = []
        for step in range(STEPS):
            for copy in pending:
                copy.wait_recv()
            halos.extend(pending)
            if step == 0:
                material = M[...]
                pole = Q[...]
                plane = lax.broadcasted_iota(jnp.int32, (planes, rows, depth), 0)
                outside = outer_row | ((plane == cx) & (gx == gx_count - 1))
                keep_e = jnp.zeros((planes, rows, depth), F32)
                drive_e = jnp.zeros((planes, rows, depth), F32)
                for entry in range(8):
                    hit = material == entry
                    keep_e = jnp.where(hit, keep_e_table[entry : entry + 1, :][None], keep_e)
                    drive_e = jnp.where(hit, drive_e_table[entry : entry + 1, :][None], drive_e)
                keep_j = jnp.zeros((planes, rows, depth), F32)
                drive_j = jnp.zeros((planes, rows, depth), F32)
                for entry in range(4):
                    hit = pole == entry
                    keep_j = jnp.where(hit, keep_j_table[entry : entry + 1, :][None], keep_j)
                    drive_j = jnp.where(hit, drive_j_table[entry : entry + 1, :][None], drive_j)
                K[0] = jnp.where(outside, 0.0, keep_e)
                K[1] = jnp.where(outside, 0.0, drive_e)
                K[2] = keep_j
                K[3] = drive_j
            hx = H[step, 0, 0:planes]
            hy = H[step, 1, 0:planes]
            hz = H[step, 2, 0:planes]
            edge_y = jnp.where(gx == 0, 0.0, H[step, 1, planes : planes + 1])
            edge_z = jnp.where(gx == 0, 0.0, H[step, 2, planes : planes + 1])
            hy_x = jnp.concatenate([edge_y, hy[0 : planes - 1]], axis=0)
            hz_x = jnp.concatenate([edge_z, hz[0 : planes - 1]], axis=0)
            curls = (
                hz - prev_y(hz) - (hy - prev_z(hy)),
                hx - prev_z(hx) - (hz - hz_x),
                hy - hy_x - (hx - prev_y(hx)),
            )
            fresh = []
            for axis in range(3):
                old = E[axis]
                flow = K[2] * J[axis] + K[3] * old
                J[axis] = flow
                value = K[0] * old + K[1] * (curls[axis] - flow)
                E[axis] = value
                fresh.append(value)
            ex, ey, ez = fresh
            ex_o, ey_o, ez_o = (value[0:cx, 0:cy] for value in fresh)
            ex_y = pltpu.roll(ex, rows - 1, 1)[0:cx, 0:cy]
            ez_y = pltpu.roll(ez, rows - 1, 1)[0:cx, 0:cy]
            ey_x = ey[1 : cx + 1, 0:cy]
            ez_x = ez[1 : cx + 1, 0:cy]
            first = ez_y - ez_o - (next_z(ey_o) - ey_o)
            second = next_z(ex_o) - ex_o - (ez_x - ez_o)
            third = ey_x - ey_o - (ex_y - ex_o)
            new_h = []
            for axis, turn in enumerate((first, second, third)):
                value = H[step, axis, 0:cx, 0:cy] - DT * turn
                if step + 1 < STEPS:
                    H[step + 1, axis, 0:cx, 0:cy] = value
                else:
                    h_out[axis] = value
                    e_out[axis] = fresh[axis][0:cx, 0:cy]
                    j_out[axis] = J[axis, 0:cx, 0:cy]
                new_h.append(value)
            if step + 1 < STEPS:
                pending = halo(step + 1)
            for index, value in enumerate((new_h[2], -new_h[0], -ez_o, ex_o)):
                S[step, index] = jnp.sum(value * face_weight, axis=1) * inside
            scatter(step)
            if step > 0:
                gather(step - 1)
        gather(STEPS - 1)

        real = [jnp.zeros((8, freqs), F32) for _ in range(8)]
        imag = [jnp.zeros((8, freqs), F32) for _ in range(8)]
        for step in range(STEPS):
            gathered(step)
            lines = jnp.dot(
                G[step].reshape(4 * gy_count, depth),
                TZ[...],
                precision=HIGHEST,
                preferred_element_type=F32,
            )
            cos_t, sin_t = sincos(omega * ((step + 1) * DT))
            for index in range(8):
                along_cos = lines[index * 8 : index * 8 + 8, 0:freqs]
                along_sin = lines[index * 8 : index * 8 + 8, freqs:]
                real[index] = real[index] + (along_cos * cos_t + along_sin * sin_t)
                imag[index] = imag[index] + (along_sin * cos_t - along_cos * sin_t)
        for index in range(8):
            A[index, 0] = real[index]
            A[index, 1] = imag[index]

        sine_theta = jnp.sqrt(1.0 - uz_own**2)
        scale = 1.0 / math.sqrt(gx_count * cx * depth)
        uz_over = uz_own / sine_theta
        inverse = 1.0 / sine_theta

        def project(tile):
            start = pl.multiple_of(tile * 8, 8)
            span = pl.ds(start, 8)
            sums = []
            for index in range(8):
                total_re = jnp.zeros((8, freqs), F32)
                total_im = jnp.zeros((8, freqs), F32)
                for cell in range(cx):
                    a_re = A[index, 0, cell : cell + 1, :]
                    a_im = A[index, 1, cell : cell + 1, :]
                    c = TX[0, cell, span, :]
                    s = TX[1, cell, span, :]
                    total_re = total_re + (a_re * c - a_im * s)
                    total_im = total_im + (a_re * s + a_im * c)
                sums.append((total_re, total_im))
            turned = []
            for comp in range(4):
                out_re = jnp.zeros((8, freqs), F32)
                out_im = jnp.zeros((8, freqs), F32)
                for face in range(2):
                    value_re, value_im = sums[comp * 2 + face]
                    c = TY[face, 0, span, :]
                    s = TY[face, 1, span, :]
                    out_re = out_re + (value_re * c - value_im * s)
                    out_im = out_im + (value_re * s + value_im * c)
                turned.append((out_re * scale, out_im * scale))
            ux_here = TX[2, 0, span, :]
            uy_here = TX[2, 1, span, :]
            ratio_a = ux_here * uz_over
            ratio_b = uy_here * inverse
            for part in range(2):
                nx, nz, lx, lz = (turned[comp][part] for comp in range(4))
                PART[part, span, :] = lx * ratio_b - nx * ratio_a + nz * sine_theta
                PART[2 + part, span, :] = lx * ratio_a - lz * sine_theta + nx * ratio_b

        TX[2, 0] = ux + jnp.zeros((dirs_x, freqs), F32)
        TX[2, 1] = uy

        def exchange(other):
            step = lax.rem(other + gx_count - gx, gx_count)
            return pltpu.make_async_remote_copy(
                src_ref=PART.at[:, pl.ds(other, 1), :],
                dst_ref=RX.at[:, pl.ds(gx, 1), :],
                send_sem=gx_send.at[step],
                recv_sem=gx_recv.at[step],
                device_id=(other, gy),
                device_id_type=MESH,
            )

        def send(other, carry):
            @pl.when(other != gx)
            def _():
                exchange(other).start()

            return carry

        def project_and_send(turn, carry):
            away = lax.div(turn + 1, 2)
            away = jnp.where(lax.rem(turn, 2) == 0, away, -away)
            tile = lax.rem(lax.div(gx, 8) + tiles // 2 + away + tiles, tiles)
            project(tile)
            lax.fori_loop(tile * 8, tile * 8 + 8, send, 0)
            return carry

        def receive(step, carry):
            exchange(lax.rem(gx + step, gx_count)).wait_recv()
            return carry

        def finish(step, carry):
            exchange(lax.rem(gx + step, gx_count)).wait_send()
            return carry

        pl.semaphore_wait(row_sem.at[0], 2)
        lax.fori_loop(0, tiles, project_and_send, 0)
        RX[:, pl.ds(gx, 1), :] = PART[:, pl.ds(gx, 1), :]
        for copy in halos:
            copy.wait_send()
        for step in range(STEPS):
            collected(step)
        lax.fori_loop(1, gx_count, receive, 0)
        far_out[...] = jnp.sum(RX[...], axis=1, keepdims=True)
        lax.fori_loop(1, gx_count, finish, 0)

    return kernel


def solution(mesh):
    gx_count = mesh.shape["gx"]
    gy_count = mesh.shape["gy"]

    def body(
        e_field,
        h_field,
        current,
        material,
        pole,
        permittivity,
        conductivity,
        plasma,
        damping,
        box,
        spectral_slot,
        ux_index,
        uz_index,
    ):
        _, cx, cy, depth = e_field.shape
        freqs = spectral_slot.shape[0]
        dirs_x = ux_index.shape[0]
        anywhere = pl.BlockSpec(memory_space=pl.ANY)
        vectors = pl.BlockSpec(memory_space=pltpu.VMEM)
        inner = pltpu.VMEM(e_field.shape, F32)
        field = jax.ShapeDtypeStruct(e_field.shape, F32)
        e_field, h_field, current, far = pl.pallas_call(
            make_kernel((gx_count, gy_count, cx, cy, depth, freqs, dirs_x)),
            out_shape=(inner, inner, inner, pltpu.VMEM((4, 1, freqs), F32)),
            in_specs=[anywhere] * 13,
            out_specs=(vectors,) * 4,
            scratch_shapes=[
                pltpu.VMEM((3, cx + 1, 2 * cy, depth), F32),
                pltpu.VMEM((STEPS, 3, cx + 2, 2 * cy, depth), F32),
                pltpu.VMEM((3, cx + 1, 2 * cy, depth), F32),
                pltpu.VMEM((cx + 1, 2 * cy, depth), jnp.int32),
                pltpu.VMEM((cx + 1, 2 * cy, depth), jnp.int32),
                pltpu.VMEM((4, cx + 1, 2 * cy, depth), F32),
                pltpu.VMEM((STEPS, 4, cx, depth), F32),
                pltpu.VMEM((STEPS, 5, 4, cx, depth), F32),
                pltpu.VMEM((STEPS, 4, 8, depth), F32),
                pltpu.VMEM((STEPS, 4, gy_count, depth), F32),
                pltpu.VMEM((8, 2, cx, freqs), F32),
                pltpu.VMEM((depth, 2 * freqs), F32),
                pltpu.VMEM((3, cx, dirs_x, freqs), F32),
                pltpu.VMEM((2, 2, dirs_x, freqs), F32),
                pltpu.VMEM((4, dirs_x, freqs), F32),
                pltpu.VMEM((4, gx_count, freqs), F32),
                pltpu.SemaphoreType.DMA((13,)),
                pltpu.SemaphoreType.DMA((STEPS, 14)),
                pltpu.SemaphoreType.DMA((STEPS, 14)),
                pltpu.SemaphoreType.DMA((STEPS, cx)),
                pltpu.SemaphoreType.DMA((STEPS, cx)),
                pltpu.SemaphoreType.DMA((STEPS, gy_count)),
                pltpu.SemaphoreType.DMA((STEPS, gy_count)),
                pltpu.SemaphoreType.DMA((gx_count,)),
                pltpu.SemaphoreType.DMA((gx_count,)),
                pltpu.SemaphoreType.REGULAR((1,)),
                pltpu.SMEM(permittivity.shape, F32),
                pltpu.SMEM(conductivity.shape, F32),
                pltpu.SMEM(plasma.shape, F32),
                pltpu.SMEM(damping.shape, F32),
                pltpu.SMEM(box.shape, jnp.int32),
                pltpu.SMEM(ux_index.shape, jnp.int32),
                pltpu.SMEM(uz_index.shape, jnp.int32),
                pltpu.VMEM((1, freqs), jnp.int32),
            ],
            compiler_params=pltpu.CompilerParams(collective_id=0, has_side_effects=True),
        )(
            e_field,
            h_field,
            current,
            material,
            pole,
            permittivity,
            conductivity,
            plasma,
            damping,
            box,
            ux_index,
            uz_index,
            spectral_slot.reshape(1, freqs),
        )
        e_field, h_field, current, far = pl.pallas_call(
            write_out,
            out_shape=(field, field, field, jax.ShapeDtypeStruct((4, 1, freqs), F32)),
            in_specs=[vectors] * 4,
            out_specs=(anywhere,) * 4,
            scratch_shapes=[pltpu.SemaphoreType.DMA((4,))],
        )(
            *(
                pltpu.with_memory_space_constraint(value, pltpu.VMEM)
                for value in (e_field, h_field, current, far)
            )
        )
        return e_field, h_field, current, far.reshape(4, 1, 1, freqs)

    fields = P(None, "gx", "gy", None)
    cells = P("gx", "gy", None)
    return jax.shard_map(
        body,
        mesh=mesh,
        in_specs=(fields, fields, fields, cells, cells) + (P(),) * 8,
        out_specs=(fields,) * 4,
        check_vma=False,
    )
```

```python
import math

import jax
import jax.numpy as jnp
from jax import lax
from jax.experimental import pallas as pl
from jax.experimental.pallas import tpu as pltpu
from jax.sharding import PartitionSpec as P

STEPS = 3
SPECTRUM_POINTS = 512
AGRID = 256
LOW_FIRST, LOW_LAST = 1, 32
HIGH_FIRST, HIGH_LAST = 96, 127
DT = 0.5
MESH = pl.DeviceIdType.MESH
F32 = jnp.float32
HIGHEST = lax.Precision.HIGHEST
TWO_OVER_PI = 0.6366197723675814
HALF_PI_HIGH = 1.5703125
HALF_PI_LOW = 4.838267948966e-4


def sincos(angle):
    turns = jnp.round(angle * TWO_OVER_PI)
    rest = (angle - turns * HALF_PI_HIGH) - turns * HALF_PI_LOW
    square = rest * rest
    sine = rest + rest * square * (
        -1.6666654611e-1 + square * (8.3321608736e-3 + square * -1.9515295891e-4)
    )
    cosine = (
        1.0
        - 0.5 * square
        + square
        * square
        * (4.166664568298827e-2 + square * (-1.388731625493765e-3 + square * 2.443315711809948e-5))
    )
    quadrant = turns.astype(jnp.int32)
    odd = (quadrant & 1) != 0
    sine_part = jnp.where(odd, cosine, sine)
    cosine_part = jnp.where(odd, sine, cosine)
    sine_out = jnp.where((quadrant & 2) != 0, -sine_part, sine_part)
    cosine_out = jnp.where(((quadrant + 1) & 2) != 0, -cosine_part, cosine_part)
    return cosine_out, sine_out


def write_out(*refs):
    sources, targets, sems = refs[0:4], refs[4:8], refs[8]
    copies = [
        pltpu.make_async_copy(source, target, sems.at[index])
        for index, (source, target) in enumerate(zip(sources, targets))
    ]
    for copy in copies:
        copy.start()
    for copy in copies:
        copy.wait()


def make_kernel(sizes):
    gx_count, gy_count, cx, cy, depth, freqs, dirs_x = sizes
    owners = 4
    share = cx // owners
    tiles = dirs_x // 8

    def kernel(
        e_in,
        h_in,
        j_in,
        m_in,
        p_in,
        permittivity_in,
        conductivity_in,
        plasma_in,
        damping_in,
        box_in,
        ux_in,
        uz_in,
        slot_in,
        e_out,
        h_out,
        j_out,
        far_out,
        E,
        H,
        J,
        M,
        Q,
        K,
        S,
        R,
        C,
        G,
        A,
        TZ,
        TX,
        TY,
        PART,
        RX,
        local_sem,
        halo_send,
        halo_recv,
        rs_send,
        rs_recv,
        ag_send,
        ag_recv,
        gx_send,
        gx_recv,
        row_sem,
        permittivity,
        conductivity,
        plasma,
        damping,
        box,
        ux_index,
        uz_index,
        slot,
    ):
        gx = lax.axis_index("gx")
        gy = lax.axis_index("gy")
        left = lax.rem(gx + gx_count - 1, gx_count)
        right = lax.rem(gx + 1, gx_count)
        below = lax.rem(gy + gy_count - 1, gy_count)
        above = lax.rem(gy + 1, gy_count)

        own = (slice(None), pl.ds(0, cx), pl.ds(0, cy))
        barrier = pltpu.get_barrier_semaphore()
        def middle_out(turn):
            away = lax.div(turn + 1, 2)
            return gy_count // 2 + jnp.where(lax.rem(turn, 2) == 0, away, -away)

        def greet_column(turn, carry):
            place = (gx, lax.rem(gy + middle_out(turn), gy_count))
            pl.semaphore_signal(barrier, inc=1, device_id=place, device_id_type=MESH)
            return carry

        def greet_row(turn, carry):
            shift = near - turn
            for place in (gx + shift, gx + gx_count - shift):
                pl.semaphore_signal(
                    barrier,
                    inc=1,
                    device_id=(lax.rem(place, gx_count), gy),
                    device_id_type=MESH,
                )
            return carry

        near = (gx_count // 2 + 1) // 2
        lax.fori_loop(0, near, greet_row, 0)
        lax.fori_loop(0, gy_count - 1, greet_column, 0)
        for place in ((left, above), (right, below)):
            pl.semaphore_signal(barrier, inc=1, device_id=place, device_id_type=MESH)

        local = [
            pltpu.make_async_copy(e_in, E.at[:, 0:cx, 0:cy, :], local_sem.at[0]),
            pltpu.make_async_copy(h_in, H.at[0, :, 0:cx, 0:cy, :], local_sem.at[1]),
            pltpu.make_async_copy(j_in, J.at[:, 0:cx, 0:cy, :], local_sem.at[2]),
            pltpu.make_async_copy(m_in, M.at[0:cx, 0:cy, :], local_sem.at[3]),
            pltpu.make_async_copy(p_in, Q.at[0:cx, 0:cy, :], local_sem.at[4]),
        ]
        small = (permittivity_in, conductivity_in, plasma_in, damping_in, box_in, ux_in, uz_in)
        held = (permittivity, conductivity, plasma, damping, box, ux_index, uz_index)
        for index, (source, target) in enumerate(zip(small, held)):
            local.append(pltpu.make_async_copy(source, target, local_sem.at[5 + index]))
        local.append(pltpu.make_async_copy(slot_in, slot, local_sem.at[12]))
        for copy in local:
            copy.start()

        pl.semaphore_wait(barrier, 2 + 2 * near + gy_count - 1)
        for place in (gx + near, gx + gx_count - near):
            pl.semaphore_signal(
                row_sem.at[0],
                inc=1,
                device_id=(lax.rem(place, gx_count), gy),
                device_id_type=MESH,
            )

        def halo(level):
            field = H.at[level]
            held = h_in if level == 0 else field
            last_x, last_y = cx - 1, cy - 1
            routes = [
                (held.at[:, 0, 0:cy, :], field.at[:, cx, 0:cy, :], (left, gy)),
                (held.at[1:3, last_x, 0:cy, :], field.at[1:3, cx + 1, 0:cy, :], (right, gy)),
                (held.at[:, 0:cx, 0, :], field.at[:, 0:cx, cy, :], (gx, below)),
                (held.at[:, 0:cx, last_y, :], field.at[:, 0:cx, 2 * cy - 1, :], (gx, above)),
                (held.at[0, 0, last_y, :], field.at[0, cx, 2 * cy - 1, :], (left, above)),
                (held.at[1, last_x, 0, :], field.at[1, cx + 1, cy, :], (right, below)),
            ]
            if level == 0:
                for source, ref in ((e_in, E), (j_in, J)):
                    routes.append((source.at[1:3, 0, :, :], ref.at[1:3, cx, 0:cy, :], (left, gy)))
                    routes.append((source.at[:, :, 0, :], ref.at[:, 0:cx, cy, :], (gx, below)))
                for source, ref in ((m_in, M), (p_in, Q)):
                    routes.append((source.at[0, :, :], ref.at[cx, 0:cy, :], (left, gy)))
                    routes.append((source.at[:, 0, :], ref.at[0:cx, cy, :], (gx, below)))
            copies = []
            for index, (source, target, place) in enumerate(routes):
                copy = pltpu.make_async_remote_copy(
                    src_ref=source,
                    dst_ref=target,
                    send_sem=halo_send.at[level, index],
                    recv_sem=halo_recv.at[level, index],
                    device_id=place,
                    device_id_type=MESH,
                )
                copy.start()
                copies.append(copy)
            return copies

        pending = halo(0)
        for copy in local:
            copy.wait()

        omega = math.pi * (slot[...].astype(F32) + 0.5) / SPECTRUM_POINTS
        uz_own = -0.7 + 1.4 * (jnp.full((1, freqs), uz_index[gy], jnp.int32).astype(F32) + 0.5) / AGRID
        place_z = (lax.broadcasted_iota(jnp.int32, (depth, freqs), 0) - depth // 2).astype(F32)
        cos_z, sin_z = sincos((omega * uz_own) * place_z)
        TZ[:, 0:freqs] = cos_z
        TZ[:, freqs:] = sin_z

        sublane = lax.broadcasted_iota(jnp.int32, (8, freqs), 0)
        ux_tiles = []
        for tile in range(tiles):
            labels = jnp.zeros((8, freqs), jnp.int32)
            for row in range(8):
                labels = jnp.where(sublane == row, ux_index[tile * 8 + row], labels)
            ux_tiles.append(labels)
        ux = -0.7 + 1.4 * (jnp.concatenate(ux_tiles, axis=0).astype(F32) + 0.5) / AGRID
        omega_ux = omega * ux

        def fill_x(cell, carry):
            place_x = jnp.full((1, 1), gx * cx + cell - (gx_count * cx) // 2, jnp.int32).astype(F32)
            cos_x, sin_x = sincos(omega_ux * place_x)
            TX[0, cell] = cos_x
            TX[1, cell] = sin_x
            return carry

        lax.fori_loop(0, cx, fill_x, 0)
        uy = jnp.sqrt(1.0 - ux**2 - uz_own**2)
        for face in range(2):
            place_y = jnp.full((1, 1), box[2 + face] - (gy_count * cy) // 2, jnp.int32).astype(F32)
            cos_y, sin_y = sincos((omega * uy) * place_y)
            TY[face, 0] = cos_y
            TY[face, 1] = sin_y

        planes, rows = cx + 1, 2 * cy
        row = lax.broadcasted_iota(jnp.int32, (1, rows, depth), 1)
        lane = lax.broadcasted_iota(jnp.int32, (1, 1, depth), 2)
        first_row = (row == 0) & (gy == 0)
        outer_row = (row >= cy) & (gy == gy_count - 1)

        def prev_y(value):
            return jnp.where(first_row, 0.0, pltpu.roll(value, 1, 1))

        def prev_z(value):
            return jnp.where(lane == 0, 0.0, pltpu.roll(value, 1, 2))

        def next_z(value):
            return jnp.where(lane == depth - 1, 0.0, pltpu.roll(value, depth - 1, 2))

        table_row = lax.broadcasted_iota(jnp.int32, (8, depth), 0)

        def table(source, count):
            values = jnp.ones((8, depth), F32)
            for entry in range(count):
                values = jnp.where(table_row == entry, source[entry], values)
            return values

        eps_table = table(permittivity, 8)
        sig_table = table(conductivity, 8)
        plasma_table = table(plasma, 4)
        damping_table = table(damping, 4)
        loss = sig_table * DT / (2.0 * eps_table)
        keep_e_table = (1.0 - loss) / (1.0 + loss)
        drive_e_table = DT / eps_table / (1.0 + loss)
        rate = damping_table * DT / 2.0
        keep_j_table = (1.0 - rate) / (1.0 + rate)
        drive_j_table = plasma_table * DT / (1.0 + rate)

        y_row = lax.broadcasted_iota(jnp.int32, (1, cy, depth), 1) + gy * cy
        face_weight = jnp.where(y_row == box[3], 1.0, 0.0) - jnp.where(y_row == box[2], 1.0, 0.0)
        x_cell = lax.broadcasted_iota(jnp.int32, (cx, depth), 0) + gx * cx
        inside = jnp.where((x_cell >= box[0]) & (x_cell < box[1]), 1.0, 0.0)

        low = gy < gy_count // 2
        base = jnp.where(low, LOW_FIRST // cy, HIGH_FIRST // cy)
        place = gy - base
        members = jnp.where(low, LOW_LAST // cy, HIGH_LAST // cy) - base + 1
        holds = (place >= 0) & (place < members)
        collects = (place >= 0) & (place < owners)
        quarter = jnp.where(low, 0, owners) + place
        slots = 1 + max(LOW_LAST // cy - LOW_FIRST // cy, HIGH_LAST // cy - HIGH_FIRST // cy)

        def to_owner(step, owner):
            cells = pl.ds(owner * share, share)
            return pltpu.make_async_remote_copy(
                src_ref=S.at[step, :, cells, :],
                dst_ref=R.at[step, place, :, cells, :],
                send_sem=rs_send.at[step, owner],
                recv_sem=rs_recv.at[step, place],
                device_id=(gx, base + owner),
                device_id_type=MESH,
            )

        def from_member(step, member):
            cells = pl.ds(place * share, share)
            return pltpu.make_async_remote_copy(
                src_ref=S.at[step, :, cells, :],
                dst_ref=R.at[step, member, :, cells, :],
                send_sem=rs_send.at[step, 0],
                recv_sem=rs_recv.at[step, member],
                device_id=(gx, base + member),
                device_id_type=MESH,
            )

        def to_column(step, offset):
            return pltpu.make_async_remote_copy(
                src_ref=C.at[step, :, pl.ds(place * share, share), :],
                dst_ref=G.at[step, :, pl.ds(quarter * share, share), :],
                send_sem=ag_send.at[step, offset],
                recv_sem=ag_recv.at[step, quarter],
                device_id=(gx, lax.rem(gy + offset, gy_count)),
                device_id_type=MESH,
            )

        def from_column(step, part):
            cells = pl.ds(part * share, share)
            return pltpu.make_async_remote_copy(
                src_ref=G.at[step, :, cells, :],
                dst_ref=G.at[step, :, cells, :],
                send_sem=ag_send.at[step, 0],
                recv_sem=ag_recv.at[step, part],
                device_id=(gx, above),
                device_id_type=MESH,
            )

        def scatter(step):
            for owner in range(owners):

                @pl.when(holds & (place != owner))
                def _():
                    to_owner(step, owner).start()

            @pl.when(collects)
            def _():
                R[step, place] = S[step]

        def gather(step):
            @pl.when(collects)
            def _():
                for member in range(slots):

                    @pl.when((place != member) & (member < members))
                    def _():
                        from_member(step, member).wait_recv()

                total = R[step, 0]
                for member in range(1, slots):
                    total = total + jnp.where(member < members, R[step, member], 0.0)
                C[step] = total

                def send_column(turn, carry):
                    to_column(step, middle_out(turn)).start()
                    return carry

                lax.fori_loop(0, gy_count - 1, send_column, 0)
                for cell in range(share):
                    G[step, :, pl.ds(quarter * share + cell, 1), :] = C[
                        step, :, pl.ds(place * share + cell, 1), :
                    ]

        def gathered(step):
            for part in range(2 * owners):
                owner = part if part < owners else HIGH_FIRST // cy + part - owners

                @pl.when(gy != owner)
                def _():
                    from_column(step, part).wait_recv()

        def collected(step):
            for owner in range(owners):

                @pl.when(holds & (place != owner))
                def _():
                    to_owner(step, owner).wait_send()

            @pl.when(collects)
            def _():

                def sent_column(offset, carry):
                    to_column(step, offset).wait_send()
                    return carry

                lax.fori_loop(1, gy_count, sent_column, 0)

        halos = []
        for step in range(STEPS):
            for copy in pending:
                copy.wait_recv()
            halos.extend(pending)
            if step == 0:
                material = M[...]
                pole = Q[...]
                plane = lax.broadcasted_iota(jnp.int32, (planes, rows, depth), 0)
                outside = outer_row | ((plane == cx) & (gx == gx_count - 1))
                keep_e = jnp.zeros((planes, rows, depth), F32)
                drive_e = jnp.zeros((planes, rows, depth), F32)
                for entry in range(8):
                    hit = material == entry
                    keep_e = jnp.where(hit, keep_e_table[entry : entry + 1, :][None], keep_e)
                    drive_e = jnp.where(hit, drive_e_table[entry : entry + 1, :][None], drive_e)
                keep_j = jnp.zeros((planes, rows, depth), F32)
                drive_j = jnp.zeros((planes, rows, depth), F32)
                for entry in range(4):
                    hit = pole == entry
                    keep_j = jnp.where(hit, keep_j_table[entry : entry + 1, :][None], keep_j)
                    drive_j = jnp.where(hit, drive_j_table[entry : entry + 1, :][None], drive_j)
                K[0] = jnp.where(outside, 0.0, keep_e)
                K[1] = jnp.where(outside, 0.0, drive_e)
                K[2] = keep_j
                K[3] = drive_j
            hx = H[step, 0, 0:planes]
            hy = H[step, 1, 0:planes]
            hz = H[step, 2, 0:planes]
            edge_y = jnp.where(gx == 0, 0.0, H[step, 1, planes : planes + 1])
            edge_z = jnp.where(gx == 0, 0.0, H[step, 2, planes : planes + 1])
            hy_x = jnp.concatenate([edge_y, hy[0 : planes - 1]], axis=0)
            hz_x = jnp.concatenate([edge_z, hz[0 : planes - 1]], axis=0)
            curls = (
                hz - prev_y(hz) - (hy - prev_z(hy)),
                hx - prev_z(hx) - (hz - hz_x),
                hy - hy_x - (hx - prev_y(hx)),
            )
            fresh = []
            for axis in range(3):
                old = E[axis]
                flow = K[2] * J[axis] + K[3] * old
                J[axis] = flow
                value = K[0] * old + K[1] * (curls[axis] - flow)
                E[axis] = value
                fresh.append(value)
            ex, ey, ez = fresh
            ex_o, ey_o, ez_o = (value[0:cx, 0:cy] for value in fresh)
            ex_y = pltpu.roll(ex, rows - 1, 1)[0:cx, 0:cy]
            ez_y = pltpu.roll(ez, rows - 1, 1)[0:cx, 0:cy]
            ey_x = ey[1 : cx + 1, 0:cy]
            ez_x = ez[1 : cx + 1, 0:cy]
            first = ez_y - ez_o - (next_z(ey_o) - ey_o)
            second = next_z(ex_o) - ex_o - (ez_x - ez_o)
            third = ey_x - ey_o - (ex_y - ex_o)
            new_h = []
            for axis, turn in enumerate((first, second, third)):
                value = H[step, axis, 0:cx, 0:cy] - DT * turn
                if step + 1 < STEPS:
                    H[step + 1, axis, 0:cx, 0:cy] = value
                new_h.append(value)
            if step + 1 < STEPS:
                pending = halo(step + 1)
            for index, value in enumerate((new_h[2], -new_h[0], -ez_o, ex_o)):
                S[step, index] = jnp.sum(value * face_weight, axis=1) * inside
            scatter(step)
            if step > 0:
                gather(step - 1)
        for axis in range(3):
            h_out[axis] = new_h[axis]
            e_out[axis] = E[axis, 0:cx, 0:cy]
            j_out[axis] = J[axis, 0:cx, 0:cy]
        gather(STEPS - 1)

        real = [jnp.zeros((8, freqs), F32) for _ in range(8)]
        imag = [jnp.zeros((8, freqs), F32) for _ in range(8)]
        for step in range(STEPS):
            gathered(step)
            lines = jnp.dot(
                G[step].reshape(4 * gy_count, depth),
                TZ[...],
                precision=HIGHEST,
                preferred_element_type=F32,
            )
            cos_t, sin_t = sincos(omega * ((step + 1) * DT))
            for index in range(8):
                along_cos = lines[index * 8 : index * 8 + 8, 0:freqs]
                along_sin = lines[index * 8 : index * 8 + 8, freqs:]
                real[index] = real[index] + (along_cos * cos_t + along_sin * sin_t)
                imag[index] = imag[index] + (along_sin * cos_t - along_cos * sin_t)
        for index in range(8):
            A[index, 0] = real[index]
            A[index, 1] = imag[index]

        sine_theta = jnp.sqrt(1.0 - uz_own**2)
        scale = 1.0 / math.sqrt(gx_count * cx * depth)
        uz_over = uz_own / sine_theta
        inverse = 1.0 / sine_theta

        def project(tile):
            start = pl.multiple_of(tile * 8, 8)
            span = pl.ds(start, 8)
            sums = []
            for index in range(8):
                total_re = jnp.zeros((8, freqs), F32)
                total_im = jnp.zeros((8, freqs), F32)
                for cell in range(cx):
                    a_re = A[index, 0, cell : cell + 1, :]
                    a_im = A[index, 1, cell : cell + 1, :]
                    c = TX[0, cell, span, :]
                    s = TX[1, cell, span, :]
                    total_re = total_re + (a_re * c - a_im * s)
                    total_im = total_im + (a_re * s + a_im * c)
                sums.append((total_re, total_im))
            turned = []
            for comp in range(4):
                out_re = jnp.zeros((8, freqs), F32)
                out_im = jnp.zeros((8, freqs), F32)
                for face in range(2):
                    value_re, value_im = sums[comp * 2 + face]
                    c = TY[face, 0, span, :]
                    s = TY[face, 1, span, :]
                    out_re = out_re + (value_re * c - value_im * s)
                    out_im = out_im + (value_re * s + value_im * c)
                turned.append((out_re * scale, out_im * scale))
            ux_here = TX[2, 0, span, :]
            uy_here = TX[2, 1, span, :]
            ratio_a = ux_here * uz_over
            ratio_b = uy_here * inverse
            for part in range(2):
                nx, nz, lx, lz = (turned[comp][part] for comp in range(4))
                PART[part, span, :] = lx * ratio_b - nx * ratio_a + nz * sine_theta
                PART[2 + part, span, :] = lx * ratio_a - lz * sine_theta + nx * ratio_b

        TX[2, 0] = ux + jnp.zeros((dirs_x, freqs), F32)
        TX[2, 1] = uy

        def exchange(other):
            step = lax.rem(other + gx_count - gx, gx_count)
            return pltpu.make_async_remote_copy(
                src_ref=PART.at[:, pl.ds(other, 1), :],
                dst_ref=RX.at[:, pl.ds(gx, 1), :],
                send_sem=gx_send.at[step],
                recv_sem=gx_recv.at[step],
                device_id=(other, gy),
                device_id_type=MESH,
            )

        def send(other, carry):
            @pl.when(other != gx)
            def _():
                exchange(other).start()

            return carry

        def project_and_send(turn, carry):
            away = lax.div(turn + 1, 2)
            away = jnp.where(lax.rem(turn, 2) == 0, away, -away)
            tile = lax.rem(lax.div(gx, 8) + tiles // 2 + away + tiles, tiles)
            project(tile)
            lax.fori_loop(tile * 8, tile * 8 + 8, send, 0)
            return carry

        def receive(step, carry):
            exchange(lax.rem(gx + step, gx_count)).wait_recv()
            return carry

        def finish(step, carry):
            exchange(lax.rem(gx + step, gx_count)).wait_send()
            return carry

        pl.semaphore_wait(row_sem.at[0], 2)
        lax.fori_loop(0, tiles, project_and_send, 0)
        RX[:, pl.ds(gx, 1), :] = PART[:, pl.ds(gx, 1), :]
        for copy in halos:
            copy.wait_send()
        for step in range(STEPS):
            collected(step)
        lax.fori_loop(1, gx_count, receive, 0)
        far_out[...] = jnp.sum(RX[...], axis=1, keepdims=True)
        lax.fori_loop(1, gx_count, finish, 0)

    return kernel


def solution(mesh):
    gx_count = mesh.shape["gx"]
    gy_count = mesh.shape["gy"]

    def body(
        e_field,
        h_field,
        current,
        material,
        pole,
        permittivity,
        conductivity,
        plasma,
        damping,
        box,
        spectral_slot,
        ux_index,
        uz_index,
    ):
        _, cx, cy, depth = e_field.shape
        freqs = spectral_slot.shape[0]
        dirs_x = ux_index.shape[0]
        anywhere = pl.BlockSpec(memory_space=pl.ANY)
        vectors = pl.BlockSpec(memory_space=pltpu.VMEM)
        inner = pltpu.VMEM(e_field.shape, F32)
        field = jax.ShapeDtypeStruct(e_field.shape, F32)
        e_field, h_field, current, far = pl.pallas_call(
            make_kernel((gx_count, gy_count, cx, cy, depth, freqs, dirs_x)),
            out_shape=(inner, inner, inner, pltpu.VMEM((4, 1, freqs), F32)),
            in_specs=[anywhere] * 13,
            out_specs=(vectors,) * 4,
            scratch_shapes=[
                pltpu.VMEM((3, cx + 1, 2 * cy, depth), F32),
                pltpu.VMEM((STEPS, 3, cx + 2, 2 * cy, depth), F32),
                pltpu.VMEM((3, cx + 1, 2 * cy, depth), F32),
                pltpu.VMEM((cx + 1, 2 * cy, depth), jnp.int32),
                pltpu.VMEM((cx + 1, 2 * cy, depth), jnp.int32),
                pltpu.VMEM((4, cx + 1, 2 * cy, depth), F32),
                pltpu.VMEM((STEPS, 4, cx, depth), F32),
                pltpu.VMEM((STEPS, 5, 4, cx, depth), F32),
                pltpu.VMEM((STEPS, 4, 8, depth), F32),
                pltpu.VMEM((STEPS, 4, gy_count, depth), F32),
                pltpu.VMEM((8, 2, cx, freqs), F32),
                pltpu.VMEM((depth, 2 * freqs), F32),
                pltpu.VMEM((3, cx, dirs_x, freqs), F32),
                pltpu.VMEM((2, 2, dirs_x, freqs), F32),
                pltpu.VMEM((4, dirs_x, freqs), F32),
                pltpu.VMEM((4, gx_count, freqs), F32),
                pltpu.SemaphoreType.DMA((13,)),
                pltpu.SemaphoreType.DMA((STEPS, 14)),
                pltpu.SemaphoreType.DMA((STEPS, 14)),
                pltpu.SemaphoreType.DMA((STEPS, cx)),
                pltpu.SemaphoreType.DMA((STEPS, cx)),
                pltpu.SemaphoreType.DMA((STEPS, gy_count)),
                pltpu.SemaphoreType.DMA((STEPS, gy_count)),
                pltpu.SemaphoreType.DMA((gx_count,)),
                pltpu.SemaphoreType.DMA((gx_count,)),
                pltpu.SemaphoreType.REGULAR((1,)),
                pltpu.SMEM(permittivity.shape, F32),
                pltpu.SMEM(conductivity.shape, F32),
                pltpu.SMEM(plasma.shape, F32),
                pltpu.SMEM(damping.shape, F32),
                pltpu.SMEM(box.shape, jnp.int32),
                pltpu.SMEM(ux_index.shape, jnp.int32),
                pltpu.SMEM(uz_index.shape, jnp.int32),
                pltpu.VMEM((1, freqs), jnp.int32),
            ],
            compiler_params=pltpu.CompilerParams(collective_id=0, has_side_effects=True),
        )(
            e_field,
            h_field,
            current,
            material,
            pole,
            permittivity,
            conductivity,
            plasma,
            damping,
            box,
            ux_index,
            uz_index,
            spectral_slot.reshape(1, freqs),
        )
        e_field, h_field, current, far = pl.pallas_call(
            write_out,
            out_shape=(field, field, field, jax.ShapeDtypeStruct((4, 1, freqs), F32)),
            in_specs=[vectors] * 4,
            out_specs=(anywhere,) * 4,
            scratch_shapes=[pltpu.SemaphoreType.DMA((4,))],
        )(
            *(
                pltpu.with_memory_space_constraint(value, pltpu.VMEM)
                for value in (e_field, h_field, current, far)
            )
        )
        return e_field, h_field, current, far.reshape(4, 1, 1, freqs)

    fields = P(None, "gx", "gy", None)
    cells = P("gx", "gy", None)
    return jax.shard_map(
        body,
        mesh=mesh,
        in_specs=(fields, fields, fields, cells, cells) + (P(),) * 8,
        out_specs=(fields,) * 4,
        check_vma=False,
    )
```
